32 devices in a mesh: groups: 2 (over y), depth: 4 (over z), heads: 2 (over x), dp: 2 (over core).
Axes of the slice: x: 2, y: 2, z: 4, core: 2. Of those that a mesh axis runs over, the one named last changes fastest.
Arguments:
- queries: bfloat16 [4, 4096, 2560], P('depth', ('groups', 'dp'), 'heads'), parts along dimension 1, may hold values from -8 to 8
- grad_out: bfloat16 [4, 4096, 2560], P('depth', ('groups', 'dp'), 'heads'), parts along dimension 1, may hold values from -6 to 6
- key_rows: bfloat16 [4096, 512], P(('groups', 'depth', 'dp'), 'heads'), parts along dimension 0, may hold values from -4 to 4
- value_rows: bfloat16 [4096, 512], P(('groups', 'depth', 'dp'), 'heads'), parts along dimension 0, may hold values from -6 to 6
- doc_starts: int32 [32], P('groups'), parts along dimension 0, may hold values from 0 to 15, as said below
Outputs:
- attn_out: bfloat16 [4, 4096, 2560], P('depth', ('groups', 'dp'), 'heads'), parts along dimension 1
- grad_queries: bfloat16 [4, 4096, 2560], P('depth', ('groups', 'dp'), 'heads'), parts along dimension 1
- grad_keys: float32 [4096, 512], P(('groups', 'depth', 'dp'), 'heads'), parts along dimension 0
- grad_values: float32 [4096, 512], P(('groups', 'depth', 'dp'), 'heads'), parts along dimension 0
The draws below stay inside these ranges and needn't reach their ends.
There are 2 independent parts, one for each index of `groups`. The reference program is written for one: setup_inputs(seed, part) draws one part's arguments, and reference() takes and returns one part's arrays. A program takes and returns all parts, laid end to end along the dimension named above; each array names one. Nothing has to cross between parts.
Inputs may be any that keep to these rules, and one draw needn't show every extreme that they name: doc_starts never falls, doc_starts[b] <= b, doc_starts[0] = 0, and the last block begins a document of its own.
All inputs are finite; a program needn't handle non-finite values.
Results may differ from the reference program's by a relative error of at most 0.02.
Values may be sent and summed in bfloat16 or wider, within the bound.
No kernel may reach another device: no remote copies, remote signals or barrier semaphores. Data moves between devices by JAX's collectives and lax.ppermute only.
A program may use at most 128 MiB of HBM per device.

```python
import jax
import jax.numpy as jnp
from jax import lax

HEADS = 20
KV_HEADS = 4
HEAD_DIM = 128
QB = 128
GROUP = 5
SEQ = 2048
LAYERS = 4


def draw_key_rows(key, part):
    base_key = jax.random.fold_in(key, 3)
    values_drawn = jnp.clip(jax.random.normal(base_key, (SEQ, KV_HEADS, HEAD_DIM), jnp.float32), -4.0, 4.0)
    return values_drawn.reshape(SEQ, KV_HEADS * HEAD_DIM).astype(jnp.bfloat16)


def draw_queries(key, part):
    base_key = jax.random.fold_in(key, 5)
    values_drawn = jnp.clip(jax.random.normal(base_key, (LAYERS, SEQ, HEADS * HEAD_DIM), jnp.float32), -4.0, 4.0)
    return values_drawn.astype(jnp.bfloat16)


def draw_doc_starts(key, part):
    block_total = SEQ // QB
    boundary = jax.random.randint(key, (block_total,), 0, 3)
    block_ids = jnp.arange(block_total, dtype=jnp.int32)
    marked = jnp.where((boundary == 0) | (block_ids == 0) | (block_ids == block_total - 1), block_ids, 0)
    return lax.cummax(marked, axis=0).astype(jnp.int32)


def block_levels(own_key, extent, split, smallest, top_value):
    def one(position, parts):
        steps = jax.random.uniform(jax.random.fold_in(jax.random.fold_in(own_key, 6), position), (parts,), jnp.float32, smallest / len(split), top_value / len(split))
        return jnp.repeat(jnp.exp(steps), extent[position] // parts).reshape((-1,) + (1,) * (len(extent) - position - 1))

    gain = one(*split[0])
    for cut in split[1:]:
        gain = gain * one(*cut)
    return gain


def noise(own_key, shape, spread, bound, shards=(), kind=jnp.bfloat16):
    result = jax.random.normal(own_key, shape, jnp.float32) * spread
    if len(shards) > 0:
        result = block_levels(own_key, shape, shards, -0.22, 0.18) * result
    return jnp.clip(result, min=-bound, max=bound).astype(kind)


def setup_inputs(seed: int = 0, part: int = 0) -> dict:
    arg_keys = jax.random.split(jax.random.key(seed), 6)
    own_keys = jax.random.split(jax.random.fold_in(arg_keys[5], part), 6)
    queries = draw_queries(jax.random.fold_in(jax.random.fold_in(arg_keys[5], part), 71), part)
    grad_out = noise(own_keys[1], (LAYERS, SEQ, HEADS * HEAD_DIM), 1.0, 6.0, ((0, 4), (1, 2), (2, 2)))
    key_rows = draw_key_rows(jax.random.fold_in(jax.random.fold_in(arg_keys[5], part), 71), part)
    value_rows = noise(own_keys[3], (SEQ, KV_HEADS * HEAD_DIM), 1.0, 6.0, ((0, 8), (1, 2)))
    doc_starts = draw_doc_starts(jax.random.fold_in(jax.random.fold_in(arg_keys[5], part), 71), part)
    return {"queries": queries, "grad_out": grad_out, "key_rows": key_rows, "value_rows": value_rows, "doc_starts": doc_starts}


NEG_FILL = -1e30


def layer_terms(layer_queries, layer_grads, key_heads, value_heads, allowed):
    seq_len = layer_queries.shape[0]
    softmax_scale = HEAD_DIM ** -0.5
    query_heads = layer_queries.astype(jnp.float32).reshape(seq_len, KV_HEADS, GROUP, HEAD_DIM)
    grad_heads = layer_grads.astype(jnp.float32).reshape(seq_len, KV_HEADS, GROUP, HEAD_DIM)
    scores = jnp.einsum("rkgd,jkd->kgrj", query_heads, key_heads) * softmax_scale
    masked = jnp.where(allowed, scores, NEG_FILL)
    row_max = jnp.max(masked, axis=-1, keepdims=True)
    exp_terms = jnp.where(allowed, jnp.exp(masked - row_max), 0.0)
    log_total = row_max + jnp.log(jnp.sum(exp_terms, axis=-1, keepdims=True))
    probabilities = jnp.where(allowed, jnp.exp(masked - log_total), 0.0)
    probs_low = lax.optimization_barrier(probabilities.astype(jnp.bfloat16)).astype(jnp.float32)
    attention = jnp.einsum("kgrj,jkd->rkgd", probs_low, value_heads).astype(jnp.bfloat16)
    row_dots = jnp.sum(grad_heads * attention.astype(jnp.float32), axis=-1)
    row_dots = jnp.transpose(row_dots, (1, 2, 0))
    prob_grads = jnp.einsum("rkgd,jkd->kgrj", grad_heads, value_heads)
    score_grads = (probabilities * (prob_grads - row_dots[..., None]) * softmax_scale).astype(jnp.bfloat16)
    score_grads = lax.optimization_barrier(score_grads).astype(jnp.float32)
    query_grad = jnp.einsum("kgrj,jkd->rkgd", score_grads, key_heads).astype(jnp.bfloat16)
    key_grad = jnp.einsum("kgrj,rkgd->jkd", score_grads, query_heads)
    value_grad = jnp.einsum("kgrj,rkgd->jkd", probs_low, grad_heads)
    return (attention.reshape(seq_len, -1), query_grad.reshape(seq_len, -1),
            key_grad.reshape(seq_len, -1), value_grad.reshape(seq_len, -1))


def reference(queries, grad_out, key_rows, value_rows, doc_starts):
    seq_len = key_rows.shape[0]
    positions = jnp.arange(seq_len, dtype=jnp.int32)
    first_key = doc_starts[positions // QB] * QB
    allowed = (positions[None, :] <= positions[:, None]) & (positions[None, :] >= first_key[:, None])
    key_heads = key_rows.astype(jnp.float32).reshape(seq_len, KV_HEADS, HEAD_DIM)
    value_heads = value_rows.astype(jnp.float32).reshape(seq_len, KV_HEADS, HEAD_DIM)

    def one_layer(layer_pair):
        return layer_terms(layer_pair[0], layer_pair[1], key_heads, value_heads, allowed)

    attention, query_grad, key_grad, value_grad = lax.map(one_layer, (queries, grad_out))
    return attention, query_grad, jnp.sum(key_grad, axis=0), jnp.sum(value_grad, axis=0)
```

```python
import functools
import math

import jax
import jax.numpy as jnp
from jax import lax
from jax.experimental import pallas as pl
from jax.experimental.pallas import tpu as pltpu
from jax.sharding import PartitionSpec as P

HEAD_DIM = 128
QB = 128
GROUP = 5
GW = GROUP * HEAD_DIM
NEG_FILL = -1e30
SCALE = HEAD_DIM ** -0.5
SCALE2 = SCALE * math.log2(math.e)
NT = (((1,), (1,)), ((), ()))
TN = (((0,), (0,)), ((), ()))
VMEM_LIMIT = 56 * 1024 * 1024


def dot(left, right, dims=(((1,), (0,)), ((), ()))):
    return lax.dot_general(left, right, dims, preferred_element_type=jnp.float32)


def first_keys(docs, block, count, axis):
    lane = lax.broadcasted_iota(jnp.int32, (1, count * QB) if axis else (count * QB, 1), axis)
    first = jnp.zeros(lane.shape, jnp.int32)
    for part in range(count):
        first = jnp.where(lane >= part * QB, docs[block + part] * QB, first)
    return first, block * QB + lane


def bias_of(key_pos, query_pos, first, upper):
    allowed = (key_pos <= query_pos) & (key_pos >= first) & (key_pos < upper)
    return jnp.where(allowed, 0.0, NEG_FILL)


def stack_heads(block):
    return jnp.concatenate([block[:, g * HEAD_DIM:(g + 1) * HEAD_DIM] for g in range(GROUP)], axis=0)


def pick(step, local_blocks, refs):
    if len(refs) == 1:
        return refs[0][...]
    return jnp.where(step < local_blocks, refs[0][...], refs[1][...])


def query_block(meta, step, local_blocks, count):
    part = step // local_blocks
    return meta[1 + part] + (step - part * local_blocks) * count


def tile_start(end, tile, width):
    return pl.multiple_of(jnp.maximum((end - width * (tile + 1)) * QB, 0), QB)


def value_kernel(local_blocks, parts, count, width, meta, docs, *refs):
    queries, refs = refs[:parts], refs[parts:]
    grads, refs = refs[:parts], refs[parts:]
    key_ref, total_ref, out_ref, value_sum, score_store = refs
    step = pl.program_id(1)
    span = width * QB
    block = query_block(meta, step, local_blocks, count)
    end = block + count
    tiles = (end - docs[block] + width - 1) // width
    query = stack_heads(pick(step, local_blocks, queries))
    grad = stack_heads(pick(step, local_blocks, grads))
    first, query_pos = first_keys(docs, block, count, 1)

    @pl.when(step == 0)
    def _():
        value_sum[...] = jnp.zeros_like(value_sum)

    def scores_of(tile):
        start = tile_start(end, tile, width)
        key_pos = start + lax.broadcasted_iota(jnp.int32, (span, 1), 0)
        bias = bias_of(key_pos, query_pos, first, (end - width * tile) * QB)
        scores = dot(key_ref[pl.ds(start, span), :], query, NT) + jnp.concatenate([bias] * GROUP, axis=1)
        return scores

    scores = scores_of(0)
    score_store[0] = scores

    def score_tile(tile, best):
        scores = scores_of(tile)
        score_store[tile] = scores
        return jnp.maximum(best, jnp.max(scores, axis=0, keepdims=True))

    best = lax.fori_loop(1, tiles, score_tile, jnp.max(scores, axis=0, keepdims=True)) * SCALE2
    weights = jnp.exp2(scores * SCALE2 - best)
    score_store[0] = weights

    def weight_tile(tile, total):
        weights = jnp.exp2(score_store[tile] * SCALE2 - best)
        score_store[tile] = weights
        return total + jnp.sum(weights, axis=0, keepdims=True)

    total = lax.fori_loop(1, tiles, weight_tile, jnp.sum(weights, axis=0, keepdims=True))
    inverse = 1.0 / total
    total_ref[...] = (best + jnp.log2(total))[None, None]

    def value_tile(tile, carry):
        start = tile_start(end, tile, width)
        low = (score_store[tile] * inverse).astype(jnp.bfloat16)
        value_sum[pl.ds(start, span), :] += dot(low, grad)
        return carry

    value_tile(0, 0)
    lax.fori_loop(1, tiles, value_tile, 0)

    @pl.when(step == pl.num_programs(1) - 1)
    def _():
        out_ref[...] = value_sum[...].astype(out_ref.dtype)


def query_kernel(local_blocks, parts, count, width, meta, docs, *refs):
    queries, refs = refs[:parts], refs[parts:]
    grads, refs = refs[:parts], refs[parts:]
    key_ref, value_ref, total_ref = refs[:3]
    refs = refs[3:]
    attns, refs = refs[:parts], refs[parts:]
    query_grads, refs = refs[:parts], refs[parts:]
    key_out, key_sum, prob_store, attn_sum, grad_sum = refs
    step = pl.program_id(1)
    span = width * QB
    rows = count * QB
    block = query_block(meta, step, local_blocks, count)
    end = block + count
    tiles = (end - docs[block] + width - 1) // width
    query = stack_heads(pick(step, local_blocks, queries))
    grad = stack_heads(pick(step, local_blocks, grads))
    first, query_pos = first_keys(docs, block, count, 0)
    total = jnp.concatenate(
        [
            jnp.transpose(jnp.broadcast_to(total_ref[0, 0, :, g * QB:(g + 1) * QB], (8, QB)))[:, :1]
            for g in range(GROUP * count)
        ],
        axis=0,
    )

    @pl.when(step == 0)
    def _():
        key_sum[...] = jnp.zeros_like(key_sum)

    def weights_of(tile):
        start = tile_start(end, tile, width)
        key_pos = start + lax.broadcasted_iota(jnp.int32, (1, span), 1)
        bias = bias_of(key_pos, query_pos, first, (end - width * tile) * QB)
        scores = dot(query, key_ref[pl.ds(start, span), :], NT) + jnp.concatenate([bias] * GROUP, axis=0)
        weights = jnp.exp2(scores * SCALE2 - total)
        prob_store[tile] = weights
        return dot(weights.astype(jnp.bfloat16), value_ref[pl.ds(start, span), :])

    attn_sum[...] = weights_of(0)

    def attn_tile(tile, carry):
        attn_sum[...] += weights_of(tile)
        return carry

    lax.fori_loop(1, tiles, attn_tile, 0)
    attn = attn_sum[...].astype(jnp.bfloat16)
    row_dots = jnp.sum(grad.astype(jnp.float32) * attn.astype(jnp.float32), axis=1, keepdims=True)

    def grad_of(tile):
        start = tile_start(end, tile, width)
        keys = key_ref[pl.ds(start, span), :]
        prob_grads = dot(grad, value_ref[pl.ds(start, span), :], NT)
        score_grads = (prob_store[tile] * (prob_grads - row_dots)).astype(jnp.bfloat16)
        key_sum[pl.ds(start, span), :] += dot(score_grads, query, TN)
        return dot(score_grads, keys)

    grad_sum[...] = grad_of(0)

    def grad_tile(tile, carry):
        grad_sum[...] += grad_of(tile)
        return carry

    lax.fori_loop(1, tiles, grad_tile, 0)
    query_grad = (grad_sum[...] * SCALE).astype(jnp.bfloat16)

    def emit(attn_ref, grad_ref):
        for g in range(GROUP):
            attn_ref[:, g * HEAD_DIM:(g + 1) * HEAD_DIM] = attn[g * rows:(g + 1) * rows]
            grad_ref[:, g * HEAD_DIM:(g + 1) * HEAD_DIM] = query_grad[g * rows:(g + 1) * rows]

    for part in range(parts):
        if parts == 1:
            emit(attns[0], query_grads[0])
        else:
            pl.when(step // local_blocks == part)(functools.partial(emit, attns[part], query_grads[part]))

    @pl.when(step == pl.num_programs(1) - 1)
    def _():
        key_out[...] = (key_sum[...] * SCALE).astype(key_out.dtype)


def row_specs(local_blocks, parts, count):
    def own(head, step, meta, docs):
        return (jnp.minimum(step, local_blocks - 1), meta[0] + head)

    def received(head, step, meta, docs):
        return (jnp.maximum(step - local_blocks, 0), head)

    return [pl.BlockSpec((count * QB, GW), own), pl.BlockSpec((count * QB, GW), received)][:parts]


def kv_spec(seq_len):
    return pl.BlockSpec((seq_len, HEAD_DIM), lambda head, step, meta, docs: (0, head))


def total_spec(count):
    return pl.BlockSpec((1, 1, 1, count * GW), lambda head, step, meta, docs: (head, step, 0, 0))


def run_value(meta, docs, queries, grads, keys, count, width):
    parts = len(queries)
    local_blocks = queries[0].shape[0] // (count * QB)
    steps = local_blocks * parts
    seq_len = keys.shape[0]
    heads = keys.shape[1] // HEAD_DIM
    span = width * QB
    return pl.pallas_call(
        functools.partial(value_kernel, local_blocks, parts, count, width),
        grid_spec=pltpu.PrefetchScalarGridSpec(
            num_scalar_prefetch=2,
            grid=(heads, steps),
            in_specs=row_specs(local_blocks, parts, count) * 2 + [kv_spec(seq_len)],
            out_specs=[total_spec(count), kv_spec(seq_len)],
            scratch_shapes=[
                pltpu.VMEM((seq_len, HEAD_DIM), jnp.float32),
                pltpu.VMEM((pl.cdiv(seq_len, span), span, count * GW), jnp.float32),
            ],
        ),
        out_shape=[
            jax.ShapeDtypeStruct((heads, steps, 1, count * GW), jnp.float32),
            jax.ShapeDtypeStruct(keys.shape, jnp.bfloat16),
        ],
        compiler_params=pltpu.CompilerParams(vmem_limit_bytes=VMEM_LIMIT),
        name="value_grad",
    )(meta, docs, *queries, *grads, keys)


def run_query(meta, docs, queries, grads, keys, values, totals, count, width):
    parts = len(queries)
    local_blocks = queries[0].shape[0] // (count * QB)
    steps = local_blocks * parts
    seq_len = keys.shape[0]
    heads = keys.shape[1] // HEAD_DIM
    span = width * QB
    rows = row_specs(local_blocks, parts, count)
    shapes = [jax.ShapeDtypeStruct(q.shape, jnp.bfloat16) for q in queries]
    outs = pl.pallas_call(
        functools.partial(query_kernel, local_blocks, parts, count, width),
        grid_spec=pltpu.PrefetchScalarGridSpec(
            num_scalar_prefetch=2,
            grid=(heads, steps),
            in_specs=rows * 2 + [kv_spec(seq_len), kv_spec(seq_len), total_spec(count)],
            out_specs=rows * 2 + [kv_spec(seq_len)],
            scratch_shapes=[
                pltpu.VMEM((seq_len, HEAD_DIM), jnp.float32),
                pltpu.VMEM((pl.cdiv(seq_len, span), count * GW, span), jnp.float32),
                pltpu.VMEM((count * GW, HEAD_DIM), jnp.float32),
                pltpu.VMEM((count * GW, HEAD_DIM), jnp.float32),
            ],
        ),
        out_shape=shapes * 2 + [jax.ShapeDtypeStruct(keys.shape, jnp.bfloat16)],
        compiler_params=pltpu.CompilerParams(vmem_limit_bytes=VMEM_LIMIT),
        name="query_grad",
    )(meta, docs, *queries, *grads, keys, values, totals)
    return outs[:parts], outs[parts:2 * parts], outs[-1]


def shift_perm(depth_count, hops):
    return [(d, (d + hops) % depth_count) for d in range(depth_count)]


def gather_depth(rows, depth_count):
    me = lax.axis_index("depth")
    count = rows.shape[0]
    full = jnp.zeros((count * depth_count, rows.shape[1]), rows.dtype)
    pieces = [(0, rows)]
    for hops in range(1, depth_count):
        pieces.append((hops, lax.ppermute(rows, "depth", shift_perm(depth_count, hops))))
    for hops, piece in pieces:
        source = lax.rem(me - hops + depth_count, depth_count)
        full = lax.dynamic_update_slice(full, piece, (source * count, 0))
    return full


def head_columns(rows, which, width):
    return lax.dynamic_slice(rows, (0, which * width), (rows.shape[0], width))


def swap_cores(array):
    return lax.ppermute(array, "dp", [(0, 1), (1, 0)])


def spread_heads(rows, core, width):
    own = head_columns(rows, core, width)
    other = swap_cores(head_columns(rows, 1 - core, width))
    first = core == 0
    return jnp.concatenate([jnp.where(first, own, other), jnp.where(first, other, own)], axis=0)


def return_terms(terms, depth_count, core):
    me = lax.axis_index("depth")
    shard = terms.shape[0] // (2 * depth_count)
    sums = [[], []]
    for hops in range(depth_count):
        target = lax.rem(me + hops, depth_count)
        for flip in range(2):
            side = core if flip == 0 else 1 - core
            piece = lax.dynamic_slice(terms, ((2 * target + side) * shard, 0), (shard, terms.shape[1]))
            if hops or flip:
                perm = [
                    (2 * d + c, 2 * ((d + hops) % depth_count) + (c ^ flip))
                    for d in range(depth_count)
                    for c in range(2)
                ]
                piece = lax.ppermute(piece, ("depth", "dp"), perm)
            sums[flip].append(piece.astype(jnp.float32))
    own, other = sum(sums[0]), sum(sums[1])
    first = core == 0
    return jnp.concatenate([jnp.where(first, own, other), jnp.where(first, other, own)], axis=1)


def by_head(queries, grad_out, key_rows, value_rows, doc_starts):
    depth_count = lax.axis_size("depth")
    core = lax.axis_index("dp")
    local_blocks = queries.shape[0] // QB
    kv_width = key_rows.shape[1] // 2
    query_width = queries.shape[1] // 2
    heads = kv_width // HEAD_DIM
    keys = gather_depth(spread_heads(key_rows, core, kv_width), depth_count)
    values = gather_depth(spread_heads(value_rows, core, kv_width), depth_count)
    query_got = swap_cores(head_columns(queries, 1 - core, query_width))
    grad_got = swap_cores(head_columns(grad_out, 1 - core, query_width))
    meta = jnp.stack([core * heads, core * local_blocks, (1 - core) * local_blocks]).astype(jnp.int32)
    query_parts = [queries, query_got]
    grad_parts = [grad_out, grad_got]
    totals, value_terms = run_value(meta, doc_starts, query_parts, grad_parts, keys, 2, 3)
    attns, query_grads, key_terms = run_query(
        meta, doc_starts, query_parts, grad_parts, keys, values, totals, 2, 3
    )
    value_grad = return_terms(value_terms, depth_count, core)
    key_grad = return_terms(key_terms, depth_count, core)
    outs = []
    for own, send in (attns, query_grads):
        outs.append(lax.dynamic_update_slice(own, swap_cores(send), (0, (1 - core) * query_width)))
    return outs[0], outs[1], key_grad, value_grad


def by_rows(queries, grad_out, key_rows, value_rows, doc_starts):
    axes = ("depth", "dp")
    block = lax.axis_index("dp") * (queries.shape[0] // QB)
    keys = lax.all_gather(key_rows, axes, axis=0, tiled=True)
    values = lax.all_gather(value_rows, axes, axis=0, tiled=True)
    meta = jnp.stack([jnp.zeros_like(block), block]).astype(jnp.int32)
    totals, value_terms = run_value(meta, doc_starts, [queries], [grad_out], keys, 2, 3)
    attns, query_grads, key_terms = run_query(
        meta, doc_starts, [queries], [grad_out], keys, values, totals, 2, 3
    )
    value_grad = lax.psum_scatter(value_terms, axes, scatter_dimension=0, tiled=True)
    key_grad = lax.psum_scatter(key_terms, axes, scatter_dimension=0, tiled=True)
    return attns[0], query_grads[0], key_grad.astype(jnp.float32), value_grad.astype(jnp.float32)


def per_device(queries, grad_out, key_rows, value_rows, doc_starts):
    kv_count = key_rows.shape[1] // HEAD_DIM
    split = lax.axis_size("dp") == 2 and kv_count % 2 == 0
    body = by_head if split else by_rows
    attn, query_grad, key_grad, value_grad = body(
        queries[0], grad_out[0], key_rows, value_rows, doc_starts
    )
    return attn[None], query_grad[None], key_grad, value_grad


def solution(mesh):
    rows = P("depth", ("groups", "dp"), "heads")
    shared = P(("groups", "depth", "dp"), "heads")
    return jax.shard_map(
        per_device,
        mesh=mesh,
        in_specs=(rows, rows, shared, shared, P("groups")),
        out_specs=(rows, rows, shared, shared),
        check_vma=False,
    )
```

```python
import functools
import math

import jax
import jax.numpy as jnp
from jax import lax
from jax.experimental import pallas as pl
from jax.experimental.pallas import tpu as pltpu
from jax.sharding import PartitionSpec as P

HEAD_DIM = 128
QB = 128
GROUP = 5
GW = GROUP * HEAD_DIM
NEG_FILL = -1e30
SCALE = HEAD_DIM ** -0.5
SCALE2 = SCALE * math.log2(math.e)
NT = (((1,), (1,)), ((), ()))
TN = (((0,), (0,)), ((), ()))
VMEM_LIMIT = 56 * 1024 * 1024


def dot(left, right, dims=(((1,), (0,)), ((), ()))):
    return lax.dot_general(left, right, dims, preferred_element_type=jnp.float32)


def first_keys(docs, block, count, axis):
    lane = lax.broadcasted_iota(jnp.int32, (1, count * QB) if axis else (count * QB, 1), axis)
    first = jnp.zeros(lane.shape, jnp.int32)
    for part in range(count):
        first = jnp.where(lane >= part * QB, docs[block + part] * QB, first)
    return first, block * QB + lane


def bias_of(key_pos, query_pos, first, upper):
    allowed = (key_pos <= query_pos) & (key_pos >= first) & (key_pos < upper)
    return jnp.where(allowed, 0.0, NEG_FILL)


def stack_heads(block):
    return jnp.concatenate([block[:, g * HEAD_DIM:(g + 1) * HEAD_DIM] for g in range(GROUP)], axis=0)


def pick(step, local_blocks, refs):
    if len(refs) == 1:
        return refs[0][...]
    return jnp.where(step < local_blocks, refs[0][...], refs[1][...])


def query_block(meta, step, local_blocks, count):
    part = step // local_blocks
    return meta[1 + part] + (step - part * local_blocks) * count


def tile_start(end, tile, width):
    return pl.multiple_of(jnp.maximum((end - width * (tile + 1)) * QB, 0), QB)


def value_kernel(local_blocks, parts, count, width, meta, docs, *refs):
    queries, refs = refs[:parts], refs[parts:]
    grads, refs = refs[:parts], refs[parts:]
    key_ref, total_ref, out_ref, value_sum, score_store = refs
    step = pl.program_id(1)
    span = width * QB
    block = query_block(meta, step, local_blocks, count)
    end = block + count
    tiles = (end - docs[block] + width - 1) // width
    query = stack_heads(pick(step, local_blocks, queries))
    grad = stack_heads(pick(step, local_blocks, grads))
    first, query_pos = first_keys(docs, block, count, 1)

    @pl.when(step == 0)
    def _():
        value_sum[...] = jnp.zeros_like(value_sum)

    def scores_of(tile):
        start = tile_start(end, tile, width)
        key_pos = start + lax.broadcasted_iota(jnp.int32, (span, 1), 0)
        bias = bias_of(key_pos, query_pos, first, (end - width * tile) * QB)
        scores = dot(key_ref[pl.ds(start, span), :], query, NT) + jnp.concatenate([bias] * GROUP, axis=1)
        return scores

    scores = scores_of(0)
    score_store[0] = scores

    def score_tile(tile, best):
        scores = scores_of(tile)
        score_store[tile] = scores
        return jnp.maximum(best, jnp.max(scores, axis=0, keepdims=True))

    best = lax.fori_loop(1, tiles, score_tile, jnp.max(scores, axis=0, keepdims=True)) * SCALE2
    weights = jnp.exp2(scores * SCALE2 - best)
    score_store[0] = weights

    def weight_tile(tile, total):
        weights = jnp.exp2(score_store[tile] * SCALE2 - best)
        score_store[tile] = weights
        return total + jnp.sum(weights, axis=0, keepdims=True)

    total = lax.fori_loop(1, tiles, weight_tile, jnp.sum(weights, axis=0, keepdims=True))
    inverse = 1.0 / total
    total_ref[...] = (best + jnp.log2(total))[None, None]

    def value_tile(tile, carry):
        start = tile_start(end, tile, width)
        low = (score_store[tile] * inverse).astype(jnp.bfloat16)
        value_sum[pl.ds(start, span), :] += dot(low, grad)
        return carry

    value_tile(0, 0)
    lax.fori_loop(1, tiles, value_tile, 0)

    @pl.when(step == pl.num_programs(1) - 1)
    def _():
        out_ref[...] = value_sum[...].astype(out_ref.dtype)


def query_kernel(local_blocks, parts, count, width, meta, docs, *refs):
    queries, refs = refs[:parts], refs[parts:]
    grads, refs = refs[:parts], refs[parts:]
    key_ref, value_ref, total_ref = refs[:3]
    refs = refs[3:]
    attns, refs = refs[:parts], refs[parts:]
    query_grads, refs = refs[:parts], refs[parts:]
    key_out, key_sum, prob_store, attn_sum, grad_sum = refs
    step = pl.program_id(1)
    span = width * QB
    rows = count * QB
    block = query_block(meta, step, local_blocks, count)
    end = block + count
    tiles = (end - docs[block] + width - 1) // width
    query = stack_heads(pick(step, local_blocks, queries))
    grad = stack_heads(pick(step, local_blocks, grads))
    first, query_pos = first_keys(docs, block, count, 0)
    total = jnp.concatenate(
        [
            jnp.transpose(jnp.broadcast_to(total_ref[0, 0, :, g * QB:(g + 1) * QB], (8, QB)))[:, :1]
            for g in range(GROUP * count)
        ],
        axis=0,
    )

    @pl.when(step == 0)
    def _():
        key_sum[...] = jnp.zeros_like(key_sum)

    def weights_of(tile):
        start = tile_start(end, tile, width)
        key_pos = start + lax.broadcasted_iota(jnp.int32, (1, span), 1)
        bias = bias_of(key_pos, query_pos, first, (end - width * tile) * QB)
        scores = dot(query, key_ref[pl.ds(start, span), :], NT) + jnp.concatenate([bias] * GROUP, axis=0)
        weights = jnp.exp2(scores * SCALE2 - total)
        prob_store[tile] = weights
        return dot(weights.astype(jnp.bfloat16), value_ref[pl.ds(start, span), :])

    attn_sum[...] = weights_of(0)

    def attn_tile(tile, carry):
        attn_sum[...] += weights_of(tile)
        return carry

    lax.fori_loop(1, tiles, attn_tile, 0)
    attn = attn_sum[...].astype(jnp.bfloat16)
    row_dots = jnp.sum(grad.astype(jnp.float32) * attn.astype(jnp.float32), axis=1, keepdims=True)

    def grad_of(tile):
        start = tile_start(end, tile, width)
        keys = key_ref[pl.ds(start, span), :]
        prob_grads = dot(grad, value_ref[pl.ds(start, span), :], NT)
        score_grads = (prob_store[tile] * (prob_grads - row_dots)).astype(jnp.bfloat16)
        key_sum[pl.ds(start, span), :] += dot(score_grads, query, TN)
        return dot(score_grads, keys)

    grad_sum[...] = grad_of(0)

    def grad_tile(tile, carry):
        grad_sum[...] += grad_of(tile)
        return carry

    lax.fori_loop(1, tiles, grad_tile, 0)
    query_grad = (grad_sum[...] * SCALE).astype(jnp.bfloat16)

    def emit(attn_ref, grad_ref):
        for g in range(GROUP):
            attn_ref[:, g * HEAD_DIM:(g + 1) * HEAD_DIM] = attn[g * rows:(g + 1) * rows]
            grad_ref[:, g * HEAD_DIM:(g + 1) * HEAD_DIM] = query_grad[g * rows:(g + 1) * rows]

    for part in range(parts):
        if parts == 1:
            emit(attns[0], query_grads[0])
        else:
            pl.when(step // local_blocks == part)(functools.partial(emit, attns[part], query_grads[part]))

    @pl.when(step == pl.num_programs(1) - 1)
    def _():
        key_out[...] = (key_sum[...] * SCALE).astype(key_out.dtype)


def row_specs(local_blocks, parts, count):
    def own(head, step, meta, docs):
        return (jnp.minimum(step, local_blocks - 1), meta[0] + head)

    def received(head, step, meta, docs):
        return (jnp.maximum(step - local_blocks, 0), head)

    return [pl.BlockSpec((count * QB, GW), own), pl.BlockSpec((count * QB, GW), received)][:parts]


def kv_spec(seq_len):
    return pl.BlockSpec((seq_len, HEAD_DIM), lambda head, step, meta, docs: (0, head))


def total_spec(count):
    return pl.BlockSpec((1, 1, 1, count * GW), lambda head, step, meta, docs: (head, step, 0, 0))


def run_value(meta, docs, queries, grads, keys, count, width):
    parts = len(queries)
    local_blocks = queries[0].shape[0] // (count * QB)
    steps = local_blocks * parts
    seq_len = keys.shape[0]
    heads = keys.shape[1] // HEAD_DIM
    span = width * QB
    return pl.pallas_call(
        functools.partial(value_kernel, local_blocks, parts, count, width),
        grid_spec=pltpu.PrefetchScalarGridSpec(
            num_scalar_prefetch=2,
            grid=(heads, steps),
            in_specs=row_specs(local_blocks, parts, count) * 2 + [kv_spec(seq_len)],
            out_specs=[total_spec(count), kv_spec(seq_len)],
            scratch_shapes=[
                pltpu.VMEM((seq_len, HEAD_DIM), jnp.float32),
                pltpu.VMEM((pl.cdiv(seq_len, span), span, count * GW), jnp.float32),
            ],
        ),
        out_shape=[
            jax.ShapeDtypeStruct((heads, steps, 1, count * GW), jnp.float32),
            jax.ShapeDtypeStruct(keys.shape, jnp.bfloat16),
        ],
        compiler_params=pltpu.CompilerParams(vmem_limit_bytes=VMEM_LIMIT),
        name="value_grad",
    )(meta, docs, *queries, *grads, keys)


def run_query(meta, docs, queries, grads, keys, values, totals, count, width):
    parts = len(queries)
    local_blocks = queries[0].shape[0] // (count * QB)
    steps = local_blocks * parts
    seq_len = keys.shape[0]
    heads = keys.shape[1] // HEAD_DIM
    span = width * QB
    rows = row_specs(local_blocks, parts, count)
    shapes = [jax.ShapeDtypeStruct(q.shape, jnp.bfloat16) for q in queries]
    outs = pl.pallas_call(
        functools.partial(query_kernel, local_blocks, parts, count, width),
        grid_spec=pltpu.PrefetchScalarGridSpec(
            num_scalar_prefetch=2,
            grid=(heads, steps),
            in_specs=rows * 2 + [kv_spec(seq_len), kv_spec(seq_len), total_spec(count)],
            out_specs=rows * 2 + [kv_spec(seq_len)],
            scratch_shapes=[
                pltpu.VMEM((seq_len, HEAD_DIM), jnp.float32),
                pltpu.VMEM((pl.cdiv(seq_len, span), count * GW, span), jnp.float32),
                pltpu.VMEM((count * GW, HEAD_DIM), jnp.float32),
                pltpu.VMEM((count * GW, HEAD_DIM), jnp.float32),
            ],
        ),
        out_shape=shapes * 2 + [jax.ShapeDtypeStruct(keys.shape, jnp.bfloat16)],
        compiler_params=pltpu.CompilerParams(vmem_limit_bytes=VMEM_LIMIT),
        name="query_grad",
    )(meta, docs, *queries, *grads, keys, values, totals)
    return outs[:parts], outs[parts:2 * parts], outs[-1]


def head_columns(rows, which, width):
    return lax.dynamic_slice(rows, (0, which * width), (rows.shape[0], width))


def swap_cores(array):
    return lax.ppermute(array, "dp", [(0, 1), (1, 0)])


def exchange(array):
    return lax.all_to_all(array, ("depth", "dp"), 0, 0, tiled=True)


def gather_heads(rows, depth_count):
    shard, width = rows.shape
    pieces = jnp.transpose(rows.reshape(shard, 2, width // 2), (1, 0, 2))
    pieces = jnp.broadcast_to(pieces[None], (depth_count,) + pieces.shape)
    full = exchange(pieces.reshape(2 * depth_count, shard, width // 2))
    return full.reshape(2 * depth_count * shard, width // 2)


def return_terms(terms, depth_count):
    shard = terms.shape[0] // (2 * depth_count)
    got = exchange(terms.reshape(2 * depth_count, shard, terms.shape[1]))
    got = got.reshape(depth_count, 2, shard, terms.shape[1])
    summed = jnp.sum(got.astype(jnp.float32), axis=0)
    return jnp.transpose(summed, (1, 0, 2)).reshape(shard, 2 * terms.shape[1])


def by_head(queries, grad_out, key_rows, value_rows, doc_starts):
    depth_count = lax.axis_size("depth")
    core = lax.axis_index("dp")
    local_blocks = queries.shape[0] // QB
    query_width = queries.shape[1] // 2
    heads = key_rows.shape[1] // (2 * HEAD_DIM)
    keys = gather_heads(key_rows, depth_count)
    values = gather_heads(value_rows, depth_count)
    query_got = swap_cores(head_columns(queries, 1 - core, query_width))
    grad_got = swap_cores(head_columns(grad_out, 1 - core, query_width))
    meta = jnp.stack([core * heads, core * local_blocks, (1 - core) * local_blocks]).astype(jnp.int32)
    query_parts = [queries, query_got]
    grad_parts = [grad_out, grad_got]
    totals, value_terms = run_value(meta, doc_starts, query_parts, grad_parts, keys, 2, 3)
    attns, query_grads, key_terms = run_query(
        meta, doc_starts, query_parts, grad_parts, keys, values, totals, 2, 3
    )
    value_grad = return_terms(value_terms, depth_count)
    key_grad = return_terms(key_terms, depth_count)
    outs = []
    for own, send in (attns, query_grads):
        outs.append(lax.dynamic_update_slice(own, swap_cores(send), (0, (1 - core) * query_width)))
    return outs[0], outs[1], key_grad, value_grad


def by_rows(queries, grad_out, key_rows, value_rows, doc_starts):
    axes = ("depth", "dp")
    block = lax.axis_index("dp") * (queries.shape[0] // QB)
    keys = lax.all_gather(key_rows, axes, axis=0, tiled=True)
    values = lax.all_gather(value_rows, axes, axis=0, tiled=True)
    meta = jnp.stack([jnp.zeros_like(block), block]).astype(jnp.int32)
    totals, value_terms = run_value(meta, doc_starts, [queries], [grad_out], keys, 2, 3)
    attns, query_grads, key_terms = run_query(
        meta, doc_starts, [queries], [grad_out], keys, values, totals, 2, 3
    )
    value_grad = lax.psum_scatter(value_terms, axes, scatter_dimension=0, tiled=True)
    key_grad = lax.psum_scatter(key_terms, axes, scatter_dimension=0, tiled=True)
    return attns[0], query_grads[0], key_grad.astype(jnp.float32), value_grad.astype(jnp.float32)


def per_device(queries, grad_out, key_rows, value_rows, doc_starts):
    kv_count = key_rows.shape[1] // HEAD_DIM
    split = lax.axis_size("dp") == 2 and kv_count % 2 == 0
    body = by_head if split else by_rows
    attn, query_grad, key_grad, value_grad = body(
        queries[0], grad_out[0], key_rows, value_rows, doc_starts
    )
    return attn[None], query_grad[None], key_grad, value_grad


def solution(mesh):
    rows = P("depth", ("groups", "dp"), "heads")
    shared = P(("groups", "depth", "dp"), "heads")
    return jax.shard_map(
        per_device,
        mesh=mesh,
        in_specs=(rows, rows, shared, shared, P("groups")),
        out_specs=(rows, rows, shared, shared),
        check_vma=False,
    )
```

```python
import functools
import math

import jax
import jax.numpy as jnp
from jax import lax
from jax.experimental import pallas as pl
from jax.experimental.pallas import tpu as pltpu
from jax.sharding import PartitionSpec as P

HEAD_DIM = 128
QB = 128
GROUP = 5
GW = GROUP * HEAD_DIM
NEG_FILL = -1e30
SCALE = HEAD_DIM ** -0.5
SCALE2 = SCALE * math.log2(math.e)
NT = (((1,), (1,)), ((), ()))
TN = (((0,), (0,)), ((), ()))
VMEM_LIMIT = 56 * 1024 * 1024


def dot(left, right, dims=(((1,), (0,)), ((), ()))):
    return lax.dot_general(left, right, dims, preferred_element_type=jnp.float32)


def stack_heads(block):
    return jnp.concatenate([block[:, g * HEAD_DIM:(g + 1) * HEAD_DIM] for g in range(GROUP)], axis=0)


def stage_rows(step, local_steps, count, refs, stacked):
    for part in range(count):
        rows = slice(part * QB, (part + 1) * QB)
        block = refs[0][rows, :]
        if len(refs) == 2:
            block = jnp.where(step < local_steps, block, refs[1][rows, :])
        stacked[part] = stack_heads(block)


def base_block(meta, step, local_steps, count):
    part = step // local_steps
    return meta[1 + part] + (step - part * local_steps) * count


def list_units(docs, base, count, width, unit_block, unit_tile):
    def add_block(part, unit):
        tiles = (base + part + width - docs[base + part]) // width

        def add_tile(tile, unit):
            unit_block[unit] = part
            unit_tile[unit] = tile
            return unit + 1

        return lax.fori_loop(0, tiles, add_tile, unit)

    return lax.fori_loop(0, count, add_block, 0)


def each_unit(units, batch, body):
    def many(index, carry):
        body([index * batch + k for k in range(batch)])
        return carry

    def single(unit, carry):
        body([unit])
        return carry

    whole = units // batch
    lax.fori_loop(0, whole, many, 0)
    lax.fori_loop(whole * batch, units, single, 0)


def tile_start(block, tile, width):
    return pl.multiple_of(jnp.maximum((block + 1 - width * (tile + 1)) * QB, 0), QB)


def tile_bias(docs, block, tile, start, width):
    key_pos = start + lax.broadcasted_iota(jnp.int32, (width * QB, QB), 0)
    query_pos = block * QB + lax.broadcasted_iota(jnp.int32, (width * QB, QB), 1)
    upper = (block + 1 - width * tile) * QB
    allowed = (key_pos <= query_pos) & (key_pos >= docs[block] * QB) & (key_pos < upper)
    bias = jnp.where(allowed, 0.0, NEG_FILL)
    return jnp.concatenate([bias] * GROUP, axis=1)


def value_kernel(local_steps, parts, count, width, batch, meta, docs, *refs):
    queries, refs = refs[:parts], refs[parts:]
    grads, refs = refs[:parts], refs[parts:]
    key_ref, total_ref, out_ref, value_sum, score_store, query, grad, best_ref, sum_ref = refs[:9]
    unit_block, unit_tile = refs[9:]
    step = pl.program_id(1)
    span = width * QB
    base = base_block(meta, step, local_steps, count)
    units = list_units(docs, base, count, width, unit_block, unit_tile)
    stage_rows(step, local_steps, count, queries, query)
    stage_rows(step, local_steps, count, grads, grad)
    best_ref[...] = jnp.full_like(best_ref, NEG_FILL)
    sum_ref[...] = jnp.zeros_like(sum_ref)

    @pl.when(step == 0)
    def _():
        value_sum[...] = jnp.zeros_like(value_sum)

    def score_units(which):
        scores = []
        for unit in which:
            part, tile = unit_block[unit], unit_tile[unit]
            start = tile_start(base + part, tile, width)
            bias = tile_bias(docs, base + part, tile, start, width)
            score = (dot(key_ref[pl.ds(start, span), :], query[part], NT) + bias) * SCALE2
            score_store[unit] = score
            scores.append(score)
        tops = [jnp.max(score, axis=0, keepdims=True) for score in scores]
        sums = [jnp.sum(jnp.exp2(score - top), axis=0, keepdims=True) for score, top in zip(scores, tops)]
        for unit, top, total in zip(which, tops, sums):
            part = unit_block[unit]
            old = best_ref[part]
            best = jnp.maximum(old, top)
            sum_ref[part] = sum_ref[part] * jnp.exp2(old - best) + total * jnp.exp2(top - best)
            best_ref[part] = best

    each_unit(units, batch, score_units)
    total_ref[0, 0] = best_ref[...] + jnp.log2(sum_ref[...])

    def value_units(which):
        terms = []
        for unit in which:
            part = unit_block[unit]
            low = jnp.exp2(score_store[unit] - total_ref[0, 0, part]).astype(jnp.bfloat16)
            terms.append(dot(low, grad[part]))
        for unit, term in zip(which, terms):
            start = tile_start(base + unit_block[unit], unit_tile[unit], width)
            value_sum[pl.ds(start, span), :] += term

    each_unit(units, batch, value_units)

    @pl.when(step == pl.num_programs(1) - 1)
    def _():
        out_ref[...] = value_sum[...].astype(out_ref.dtype)


def query_kernel(local_steps, parts, count, width, batch, meta, docs, *refs):
    queries, refs = refs[:parts], refs[parts:]
    grads, refs = refs[:parts], refs[parts:]
    key_ref, value_ref, total_ref = refs[:3]
    refs = refs[3:]
    attns, refs = refs[:parts], refs[parts:]
    query_grads, refs = refs[:parts], refs[parts:]
    key_out, key_sum, weight_store, dot_store, query, grad, attn_sum, grad_sum, dots_ref = refs[:9]
    unit_block, unit_tile = refs[9:]
    step = pl.program_id(1)
    span = width * QB
    base = base_block(meta, step, local_steps, count)
    units = list_units(docs, base, count, width, unit_block, unit_tile)
    stage_rows(step, local_steps, count, queries, query)
    stage_rows(step, local_steps, count, grads, grad)
    attn_sum[...] = jnp.zeros_like(attn_sum)
    grad_sum[...] = jnp.zeros_like(grad_sum)
    dots_ref[...] = jnp.zeros_like(dots_ref)

    @pl.when(step == 0)
    def _():
        key_sum[...] = jnp.zeros_like(key_sum)

    def attn_units(which):
        results = []
        for unit in which:
            part, tile = unit_block[unit], unit_tile[unit]
            start = tile_start(base + part, tile, width)
            bias = tile_bias(docs, base + part, tile, start, width)
            scores = dot(key_ref[pl.ds(start, span), :], query[part], NT) + bias
            weights = jnp.exp2(scores * SCALE2 - total_ref[0, 0, part])
            low = weights.astype(jnp.bfloat16)
            weight_store[unit] = low
            values = value_ref[pl.ds(start, span), :]
            prob_grads = dot(values, grad[part], NT)
            dot_store[unit] = prob_grads
            results.append((dot(low, values, TN), jnp.sum(weights * prob_grads, axis=0, keepdims=True)))
        for unit, (attn, dots) in zip(which, results):
            part = unit_block[unit]
            attn_sum[part] += attn
            dots_ref[part] += dots

    each_unit(units, batch, attn_units)

    def grad_units(which):
        results = []
        for unit in which:
            part = unit_block[unit]
            start = tile_start(base + part, unit_tile[unit], width)
            score_grads = weight_store[unit].astype(jnp.float32) * (dot_store[unit] - dots_ref[part])
            score_grads = score_grads.astype(jnp.bfloat16)
            results.append((
                dot(score_grads, key_ref[pl.ds(start, span), :], TN),
                dot(score_grads, query[part]),
            ))
        for unit, (query_term, key_term) in zip(which, results):
            part = unit_block[unit]
            start = tile_start(base + part, unit_tile[unit], width)
            grad_sum[part] += query_term
            key_sum[pl.ds(start, span), :] += key_term

    each_unit(units, batch, grad_units)

    def emit(attn_ref, grad_ref):
        for part in range(count):
            rows = slice(part * QB, (part + 1) * QB)
            for g in range(GROUP):
                head = slice(g * HEAD_DIM, (g + 1) * HEAD_DIM)
                stacked = slice(g * QB, (g + 1) * QB)
                attn_ref[rows, head] = attn_sum[part, stacked].astype(jnp.bfloat16)
                grad_ref[rows, head] = (grad_sum[part, stacked] * SCALE).astype(jnp.bfloat16)

    for part in range(parts):
        if parts == 1:
            emit(attns[0], query_grads[0])
        else:
            pl.when(step // local_steps == part)(functools.partial(emit, attns[part], query_grads[part]))

    @pl.when(step == pl.num_programs(1) - 1)
    def _():
        key_out[...] = (key_sum[...] * SCALE).astype(key_out.dtype)


def max_units(seq_len, count, width):
    blocks = seq_len // QB
    return sum(-(-(blocks - k) // width) for k in range(count))


def row_specs(local_steps, parts, count):
    def own(head, step, meta, docs):
        return (jnp.minimum(step, local_steps - 1), meta[0] + head)

    def received(head, step, meta, docs):
        return (jnp.maximum(step - local_steps, 0), head)

    return [pl.BlockSpec((count * QB, GW), own), pl.BlockSpec((count * QB, GW), received)][:parts]


def kv_spec(seq_len):
    return pl.BlockSpec((seq_len, HEAD_DIM), lambda head, step, meta, docs: (0, head))


def total_spec(count):
    return pl.BlockSpec((1, 1, count, 1, GW), lambda head, step, meta, docs: (head, step, 0, 0, 0))


def run_value(meta, docs, queries, grads, keys, count, width, batch):
    parts = len(queries)
    local_steps = queries[0].shape[0] // (count * QB)
    steps = local_steps * parts
    seq_len = keys.shape[0]
    heads = keys.shape[1] // HEAD_DIM
    units = max_units(seq_len, count, width)
    return pl.pallas_call(
        functools.partial(value_kernel, local_steps, parts, count, width, batch),
        grid_spec=pltpu.PrefetchScalarGridSpec(
            num_scalar_prefetch=2,
            grid=(heads, steps),
            in_specs=row_specs(local_steps, parts, count) * 2 + [kv_spec(seq_len)],
            out_specs=[total_spec(count), kv_spec(seq_len)],
            scratch_shapes=[
                pltpu.VMEM((seq_len, HEAD_DIM), jnp.float32),
                pltpu.VMEM((units, width * QB, GW), jnp.float32),
                pltpu.VMEM((count, GW, HEAD_DIM), jnp.bfloat16),
                pltpu.VMEM((count, GW, HEAD_DIM), jnp.bfloat16),
                pltpu.VMEM((count, 1, GW), jnp.float32),
                pltpu.VMEM((count, 1, GW), jnp.float32),
                pltpu.SMEM((units,), jnp.int32),
                pltpu.SMEM((units,), jnp.int32),
            ],
        ),
        out_shape=[
            jax.ShapeDtypeStruct((heads, steps, count, 1, GW), jnp.float32),
            jax.ShapeDtypeStruct(keys.shape, jnp.bfloat16),
        ],
        compiler_params=pltpu.CompilerParams(vmem_limit_bytes=VMEM_LIMIT),
        name="value_grad",
    )(meta, docs, *queries, *grads, keys)


def run_query(meta, docs, queries, grads, keys, values, totals, count, width, batch):
    parts = len(queries)
    local_steps = queries[0].shape[0] // (count * QB)
    steps = local_steps * parts
    seq_len = keys.shape[0]
    heads = keys.shape[1] // HEAD_DIM
    units = max_units(seq_len, count, width)
    rows = row_specs(local_steps, parts, count)
    shapes = [jax.ShapeDtypeStruct(q.shape, jnp.bfloat16) for q in queries]
    outs = pl.pallas_call(
        functools.partial(query_kernel, local_steps, parts, count, width, batch),
        grid_spec=pltpu.PrefetchScalarGridSpec(
            num_scalar_prefetch=2,
            grid=(heads, steps),
            in_specs=rows * 2 + [kv_spec(seq_len), kv_spec(seq_len), total_spec(count)],
            out_specs=rows * 2 + [kv_spec(seq_len)],
            scratch_shapes=[
                pltpu.VMEM((seq_len, HEAD_DIM), jnp.float32),
                pltpu.VMEM((units, width * QB, GW), jnp.bfloat16),
                pltpu.VMEM((units, width * QB, GW), jnp.float32),
                pltpu.VMEM((count, GW, HEAD_DIM), jnp.bfloat16),
                pltpu.VMEM((count, GW, HEAD_DIM), jnp.bfloat16),
                pltpu.VMEM((count, GW, HEAD_DIM), jnp.float32),
                pltpu.VMEM((count, GW, HEAD_DIM), jnp.float32),
                pltpu.VMEM((count, 1, GW), jnp.float32),
                pltpu.SMEM((units,), jnp.int32),
                pltpu.SMEM((units,), jnp.int32),
            ],
        ),
        out_shape=shapes * 2 + [jax.ShapeDtypeStruct(keys.shape, jnp.bfloat16)],
        compiler_params=pltpu.CompilerParams(vmem_limit_bytes=VMEM_LIMIT),
        name="query_grad",
    )(meta, docs, *queries, *grads, keys, values, totals)
    return outs[:parts], outs[parts:2 * parts], outs[-1]


def head_columns(rows, which, width):
    return lax.dynamic_slice(rows, (0, which * width), (rows.shape[0], width))


def swap_cores(array):
    return lax.ppermute(array, "dp", [(0, 1), (1, 0)])


def exchange(array):
    return lax.all_to_all(array, ("depth", "dp"), 0, 0, tiled=True)


def gather_heads(rows, depth_count):
    shard, width = rows.shape
    pieces = jnp.transpose(rows.reshape(shard, 2, width // 2), (1, 0, 2))
    pieces = jnp.broadcast_to(pieces[None], (depth_count,) + pieces.shape)
    full = exchange(pieces.reshape(2 * depth_count, shard, width // 2))
    return full.reshape(2 * depth_count * shard, width // 2)


def return_terms(terms, depth_count):
    shard = terms.shape[0] // (2 * depth_count)
    got = exchange(terms.reshape(2 * depth_count, shard, terms.shape[1]))
    got = got.reshape(depth_count, 2, shard, terms.shape[1])
    summed = jnp.sum(got.astype(jnp.float32), axis=0)
    return jnp.transpose(summed, (1, 0, 2)).reshape(shard, 2 * terms.shape[1])


def by_head(queries, grad_out, key_rows, value_rows, doc_starts):
    depth_count = lax.axis_size("depth")
    core = lax.axis_index("dp")
    local_blocks = queries.shape[0] // QB
    query_width = queries.shape[1] // 2
    heads = key_rows.shape[1] // (2 * HEAD_DIM)
    keys = gather_heads(key_rows, depth_count)
    values = gather_heads(value_rows, depth_count)
    query_got = swap_cores(head_columns(queries, 1 - core, query_width))
    grad_got = swap_cores(head_columns(grad_out, 1 - core, query_width))
    meta = jnp.stack([core * heads, core * local_blocks, (1 - core) * local_blocks]).astype(jnp.int32)
    query_parts = [queries, query_got]
    grad_parts = [grad_out, grad_got]
    totals, value_terms = run_value(meta, doc_starts, query_parts, grad_parts, keys, 4, 2, 4)
    attns, query_grads, key_terms = run_query(
        meta, doc_starts, query_parts, grad_parts, keys, values, totals, 4, 2, 4
    )
    value_grad = return_terms(value_terms, depth_count)
    key_grad = return_terms(key_terms, depth_count)
    outs = []
    for own, send in (attns, query_grads):
        outs.append(lax.dynamic_update_slice(own, swap_cores(send), (0, (1 - core) * query_width)))
    return outs[0], outs[1], key_grad, value_grad


def by_rows(queries, grad_out, key_rows, value_rows, doc_starts):
    axes = ("depth", "dp")
    block = lax.axis_index("dp") * (queries.shape[0] // QB)
    keys = lax.all_gather(key_rows, axes, axis=0, tiled=True)
    values = lax.all_gather(value_rows, axes, axis=0, tiled=True)
    meta = jnp.stack([jnp.zeros_like(block), block]).astype(jnp.int32)
    totals, value_terms = run_value(meta, doc_starts, [queries], [grad_out], keys, 4, 2, 4)
    attns, query_grads, key_terms = run_query(
        meta, doc_starts, [queries], [grad_out], keys, values, totals, 4, 2, 4
    )
    value_grad = lax.psum_scatter(value_terms, axes, scatter_dimension=0, tiled=True)
    key_grad = lax.psum_scatter(key_terms, axes, scatter_dimension=0, tiled=True)
    return attns[0], query_grads[0], key_grad.astype(jnp.float32), value_grad.astype(jnp.float32)


def per_device(queries, grad_out, key_rows, value_rows, doc_starts):
    kv_count = key_rows.shape[1] // HEAD_DIM
    split = lax.axis_size("dp") == 2 and kv_count % 2 == 0
    body = by_head if split else by_rows
    attn, query_grad, key_grad, value_grad = body(
        queries[0], grad_out[0], key_rows, value_rows, doc_starts
    )
    return attn[None], query_grad[None], key_grad, value_grad


def solution(mesh):
    rows = P("depth", ("groups", "dp"), "heads")
    shared = P(("groups", "depth", "dp"), "heads")
    return jax.shard_map(
        per_device,
        mesh=mesh,
        in_specs=(rows, rows, shared, shared, P("groups")),
        out_specs=(rows, rows, shared, shared),
        check_vma=False,
    )
```

```python
import functools
import math

import jax
import jax.numpy as jnp
from jax import lax
from jax.experimental import pallas as pl
from jax.experimental.pallas import tpu as pltpu
from jax.sharding import PartitionSpec as P

HEAD_DIM = 128
QB = 128
GROUP = 5
GW = GROUP * HEAD_DIM
NEG_FILL = -1e30
SCALE = HEAD_DIM ** -0.5
SCALE2 = SCALE * math.log2(math.e)
NT = (((1,), (1,)), ((), ()))
TN = (((0,), (0,)), ((), ()))
VMEM_LIMIT = 56 * 1024 * 1024


def dot(left, right, dims=(((1,), (0,)), ((), ()))):
    return lax.dot_general(left, right, dims, preferred_element_type=jnp.float32)


def stack_heads(block):
    return jnp.concatenate([block[:, g * HEAD_DIM:(g + 1) * HEAD_DIM] for g in range(GROUP)], axis=0)


def stage_rows(step, local_steps, count, refs, stacked):
    for part in range(count):
        rows = slice(part * QB, (part + 1) * QB)
        block = refs[0][rows, :]
        if len(refs) == 2:
            block = jnp.where(step < local_steps, block, refs[1][rows, :])
        stacked[part] = stack_heads(block)


def base_block(meta, step, local_steps, count):
    part = step // local_steps
    return meta[1 + part] + (step - part * local_steps) * count


def list_units(docs, base, count, width, unit_block, unit_tile):
    def add_block(part, unit):
        tiles = (base + part + width - docs[base + part]) // width

        def add_tile(tile, unit):
            unit_block[unit] = part
            unit_tile[unit] = tile
            return unit + 1

        return lax.fori_loop(0, tiles, add_tile, unit)

    return lax.fori_loop(0, count, add_block, 0)


def each_unit(units, batch, body):
    def many(index, carry):
        body([index * batch + k for k in range(batch)])
        return carry

    def single(unit, carry):
        body([unit])
        return carry

    whole = units // batch
    lax.fori_loop(0, whole, many, 0)
    lax.fori_loop(whole * batch, units, single, 0)


def tile_start(block, tile, width):
    return pl.multiple_of(jnp.maximum((block + 1 - width * (tile + 1)) * QB, 0), QB)


def tile_bias(docs, block, tile, start, width):
    key_pos = start + lax.broadcasted_iota(jnp.int32, (width * QB, QB), 0)
    query_pos = block * QB + lax.broadcasted_iota(jnp.int32, (width * QB, QB), 1)
    upper = (block + 1 - width * tile) * QB
    allowed = (key_pos <= query_pos) & (key_pos >= docs[block] * QB) & (key_pos < upper)
    bias = jnp.where(allowed, 0.0, NEG_FILL)
    return jnp.concatenate([bias] * GROUP, axis=1)


def value_kernel(local_steps, parts, count, width, batch, meta, docs, *refs):
    queries, refs = refs[:parts], refs[parts:]
    grads, refs = refs[:parts], refs[parts:]
    key_ref, total_ref, out_ref, value_sum, score_store, query, grad, best_ref, sum_ref = refs[:9]
    unit_block, unit_tile = refs[9:]
    step = pl.program_id(1)
    span = width * QB
    base = base_block(meta, step, local_steps, count)
    units = list_units(docs, base, count, width, unit_block, unit_tile)
    stage_rows(step, local_steps, count, queries, query)
    stage_rows(step, local_steps, count, grads, grad)
    best_ref[...] = jnp.full_like(best_ref, NEG_FILL)
    sum_ref[...] = jnp.zeros_like(sum_ref)

    @pl.when(step == 0)
    def _():
        value_sum[...] = jnp.zeros_like(value_sum)

    def score_units(which):
        scores = []
        for unit in which:
            part, tile = unit_block[unit], unit_tile[unit]
            start = tile_start(base + part, tile, width)
            bias = tile_bias(docs, base + part, tile, start, width)
            score = (dot(key_ref[pl.ds(start, span), :], query[part], NT) + bias) * SCALE2
            score_store[unit] = score
            scores.append(score)
        tops = [jnp.max(score, axis=0, keepdims=True) for score in scores]
        sums = [jnp.sum(jnp.exp2(score - top), axis=0, keepdims=True) for score, top in zip(scores, tops)]
        for unit, top, total in zip(which, tops, sums):
            part = unit_block[unit]
            old = best_ref[part]
            best = jnp.maximum(old, top)
            sum_ref[part] = sum_ref[part] * jnp.exp2(old - best) + total * jnp.exp2(top - best)
            best_ref[part] = best

    each_unit(units, batch, score_units)
    total_ref[0, 0] = best_ref[...] + jnp.log2(sum_ref[...])

    def value_units(which):
        terms = []
        for unit in which:
            part = unit_block[unit]
            low = jnp.exp2(score_store[unit] - total_ref[0, 0, part]).astype(jnp.bfloat16)
            terms.append(dot(low, grad[part]))
        for unit, term in zip(which, terms):
            start = tile_start(base + unit_block[unit], unit_tile[unit], width)
            value_sum[pl.ds(start, span), :] += term

    each_unit(units, batch, value_units)

    @pl.when(step == pl.num_programs(1) - 1)
    def _():
        out_ref[...] = value_sum[...].astype(out_ref.dtype)


def query_kernel(local_steps, parts, count, width, batch, meta, docs, *refs):
    queries, refs = refs[:parts], refs[parts:]
    grads, refs = refs[:parts], refs[parts:]
    key_ref, value_ref, total_ref = refs[:3]
    refs = refs[3:]
    attns, refs = refs[:parts], refs[parts:]
    query_grads, refs = refs[:parts], refs[parts:]
    key_out, key_sum, weight_store, dot_store, query, grad, attn_sum, grad_sum, dots_ref = refs[:9]
    unit_block, unit_tile = refs[9:]
    step = pl.program_id(1)
    span = width * QB
    base = base_block(meta, step, local_steps, count)
    units = list_units(docs, base, count, width, unit_block, unit_tile)
    stage_rows(step, local_steps, count, queries, query)
    stage_rows(step, local_steps, count, grads, grad)
    attn_sum[...] = jnp.zeros_like(attn_sum)
    grad_sum[...] = jnp.zeros_like(grad_sum)
    dots_ref[...] = jnp.zeros_like(dots_ref)

    @pl.when(step == 0)
    def _():
        key_sum[...] = jnp.zeros_like(key_sum)

    def attn_units(which):
        results = []
        for unit in which:
            part, tile = unit_block[unit], unit_tile[unit]
            start = tile_start(base + part, tile, width)
            bias = tile_bias(docs, base + part, tile, start, width)
            scores = dot(key_ref[pl.ds(start, span), :], query[part], NT) + bias
            weights = jnp.exp2(scores * SCALE2 - total_ref[0, 0, part])
            low = weights.astype(jnp.bfloat16)
            weight_store[unit] = low
            values = value_ref[pl.ds(start, span), :]
            prob_grads = dot(values, grad[part], NT)
            dot_store[unit] = prob_grads
            results.append((dot(low, values, TN), jnp.sum(weights * prob_grads, axis=0, keepdims=True)))
        for unit, (attn, dots) in zip(which, results):
            part = unit_block[unit]
            attn_sum[part] += attn
            dots_ref[part] += dots

    each_unit(units, batch, attn_units)

    def grad_units(which):
        results = []
        for unit in which:
            part = unit_block[unit]
            start = tile_start(base + part, unit_tile[unit], width)
            score_grads = weight_store[unit].astype(jnp.float32) * (dot_store[unit] - dots_ref[part])
            score_grads = score_grads.astype(jnp.bfloat16)
            results.append((
                dot(score_grads, key_ref[pl.ds(start, span), :], TN),
                dot(score_grads, query[part]),
            ))
        for unit, (query_term, key_term) in zip(which, results):
            part = unit_block[unit]
            start = tile_start(base + part, unit_tile[unit], width)
            grad_sum[part] += query_term
            key_sum[pl.ds(start, span), :] += key_term

    each_unit(units, batch, grad_units)

    def emit(attn_ref, grad_ref):
        for part in range(count):
            rows = slice(part * QB, (part + 1) * QB)
            for g in range(GROUP):
                head = slice(g * HEAD_DIM, (g + 1) * HEAD_DIM)
                stacked = slice(g * QB, (g + 1) * QB)
                attn_ref[rows, head] = attn_sum[part, stacked].astype(jnp.bfloat16)
                grad_ref[rows, head] = (grad_sum[part, stacked] * SCALE).astype(jnp.bfloat16)

    for part in range(parts):
        if parts == 1:
            emit(attns[0], query_grads[0])
        else:
            pl.when(step // local_steps == part)(functools.partial(emit, attns[part], query_grads[part]))

    @pl.when(step == pl.num_programs(1) - 1)
    def _():
        key_out[...] = (key_sum[...] * SCALE).astype(key_out.dtype)


def max_units(seq_len, count, width):
    blocks = seq_len // QB
    return sum(-(-(blocks - k) // width) for k in range(count))


def row_specs(local_steps, parts, count):
    def own(head, step, meta, docs):
        return (jnp.minimum(step, local_steps - 1), meta[0] + head)

    def received(head, step, meta, docs):
        return (jnp.maximum(step - local_steps, 0), head)

    return [pl.BlockSpec((count * QB, GW), own), pl.BlockSpec((count * QB, GW), received)][:parts]


def kv_spec(seq_len):
    return pl.BlockSpec((seq_len, HEAD_DIM), lambda head, step, meta, docs: (0, head))


def total_spec(count):
    return pl.BlockSpec((1, 1, count, 1, GW), lambda head, step, meta, docs: (head, step, 0, 0, 0))


def run_value(meta, docs, queries, grads, keys, count, width, batch):
    parts = len(queries)
    local_steps = queries[0].shape[0] // (count * QB)
    steps = local_steps * parts
    seq_len = keys.shape[0]
    heads = keys.shape[1] // HEAD_DIM
    units = max_units(seq_len, count, width)
    return pl.pallas_call(
        functools.partial(value_kernel, local_steps, parts, count, width, batch),
        grid_spec=pltpu.PrefetchScalarGridSpec(
            num_scalar_prefetch=2,
            grid=(heads, steps),
            in_specs=row_specs(local_steps, parts, count) * 2 + [kv_spec(seq_len)],
            out_specs=[total_spec(count), kv_spec(seq_len)],
            scratch_shapes=[
                pltpu.VMEM((seq_len, HEAD_DIM), jnp.float32),
                pltpu.VMEM((units, width * QB, GW), jnp.float32),
                pltpu.VMEM((count, GW, HEAD_DIM), jnp.bfloat16),
                pltpu.VMEM((count, GW, HEAD_DIM), jnp.bfloat16),
                pltpu.VMEM((count, 1, GW), jnp.float32),
                pltpu.VMEM((count, 1, GW), jnp.float32),
                pltpu.SMEM((units,), jnp.int32),
                pltpu.SMEM((units,), jnp.int32),
            ],
        ),
        out_shape=[
            jax.ShapeDtypeStruct((heads, steps, count, 1, GW), jnp.float32),
            jax.ShapeDtypeStruct(keys.shape, jnp.bfloat16),
        ],
        compiler_params=pltpu.CompilerParams(vmem_limit_bytes=VMEM_LIMIT),
        name="value_grad",
    )(meta, docs, *queries, *grads, keys)


def run_query(meta, docs, queries, grads, keys, values, totals, count, width, batch):
    parts = len(queries)
    local_steps = queries[0].shape[0] // (count * QB)
    steps = local_steps * parts
    seq_len = keys.shape[0]
    heads = keys.shape[1] // HEAD_DIM
    units = max_units(seq_len, count, width)
    rows = row_specs(local_steps, parts, count)
    shapes = [jax.ShapeDtypeStruct(q.shape, jnp.bfloat16) for q in queries]
    outs = pl.pallas_call(
        functools.partial(query_kernel, local_steps, parts, count, width, batch),
        grid_spec=pltpu.PrefetchScalarGridSpec(
            num_scalar_prefetch=2,
            grid=(heads, steps),
            in_specs=rows * 2 + [kv_spec(seq_len), kv_spec(seq_len), total_spec(count)],
            out_specs=rows * 2 + [kv_spec(seq_len)],
            scratch_shapes=[
                pltpu.VMEM((seq_len, HEAD_DIM), jnp.float32),
                pltpu.VMEM((units, width * QB, GW), jnp.bfloat16),
                pltpu.VMEM((units, width * QB, GW), jnp.float32),
                pltpu.VMEM((count, GW, HEAD_DIM), jnp.bfloat16),
                pltpu.VMEM((count, GW, HEAD_DIM), jnp.bfloat16),
                pltpu.VMEM((count, GW, HEAD_DIM), jnp.float32),
                pltpu.VMEM((count, GW, HEAD_DIM), jnp.float32),
                pltpu.VMEM((count, 1, GW), jnp.float32),
                pltpu.SMEM((units,), jnp.int32),
                pltpu.SMEM((units,), jnp.int32),
            ],
        ),
        out_shape=shapes * 2 + [jax.ShapeDtypeStruct(keys.shape, jnp.bfloat16)],
        compiler_params=pltpu.CompilerParams(vmem_limit_bytes=VMEM_LIMIT),
        name="query_grad",
    )(meta, docs, *queries, *grads, keys, values, totals)
    return outs[:parts], outs[parts:2 * parts], outs[-1]


def head_columns(rows, which, width):
    return lax.dynamic_slice(rows, (0, which * width), (rows.shape[0], width))


def swap_cores(array):
    return lax.ppermute(array, "dp", [(0, 1), (1, 0)])


def exchange(array):
    return lax.all_to_all(array, ("depth", "dp"), 0, 0, tiled=True)


def pack_heads(rows, depth_count):
    shard, width = rows.shape
    sides = jnp.transpose(rows.reshape(shard, 2, width // 2), (1, 0, 2))
    sides = jnp.broadcast_to(sides[None], (depth_count,) + sides.shape)
    return sides.reshape(2 * depth_count, shard, width // 2)


def unpack_rows(pieces):
    return pieces.reshape(pieces.shape[0] * pieces.shape[1], pieces.shape[2])


def return_terms(terms, depth_count):
    shard = terms.shape[0] // (2 * depth_count)
    return exchange(terms.reshape(2 * depth_count, shard, terms.shape[1]))


def add_terms(got):
    heads = [jnp.sum(got[side::2].astype(jnp.float32), axis=0) for side in range(2)]
    return jnp.concatenate(heads, axis=1)


def by_head(queries, grad_out, key_rows, value_rows, doc_starts):
    depth_count = lax.axis_size("depth")
    core = lax.axis_index("dp")
    local_blocks = queries.shape[0] // QB
    query_width = queries.shape[1] // 2
    heads = key_rows.shape[1] // (2 * HEAD_DIM)
    keys = unpack_rows(exchange(pack_heads(key_rows, depth_count)))
    values = unpack_rows(exchange(pack_heads(value_rows, depth_count)))
    meta = jnp.stack([core * heads, core * local_blocks, (1 - core) * local_blocks]).astype(jnp.int32)
    query_got = swap_cores(head_columns(queries, 1 - core, query_width))
    grad_got = swap_cores(head_columns(grad_out, 1 - core, query_width))
    query_parts = [queries, query_got]
    grad_parts = [grad_out, grad_got]
    totals, value_terms = run_value(meta, doc_starts, query_parts, grad_parts, keys, 4, 2, 4)
    value_back = return_terms(value_terms, depth_count)
    attns, query_grads, key_terms = run_query(
        meta, doc_starts, query_parts, grad_parts, keys, values, totals, 4, 2, 4
    )
    key_back = return_terms(key_terms, depth_count)
    outs = [
        lax.dynamic_update_slice(own, swap_cores(send), (0, (1 - core) * query_width))
        for own, send in (attns, query_grads)
    ]
    outs, value_grad, key_back = lax.optimization_barrier((outs, add_terms(value_back), key_back))
    return outs[0], outs[1], add_terms(key_back), value_grad


def by_rows(queries, grad_out, key_rows, value_rows, doc_starts):
    axes = ("depth", "dp")
    block = lax.axis_index("dp") * (queries.shape[0] // QB)
    keys = lax.all_gather(key_rows, axes, axis=0, tiled=True)
    values = lax.all_gather(value_rows, axes, axis=0, tiled=True)
    meta = jnp.stack([jnp.zeros_like(block), block]).astype(jnp.int32)
    totals, value_terms = run_value(meta, doc_starts, [queries], [grad_out], keys, 4, 2, 4)
    attns, query_grads, key_terms = run_query(
        meta, doc_starts, [queries], [grad_out], keys, values, totals, 4, 2, 4
    )
    value_grad = lax.psum_scatter(value_terms, axes, scatter_dimension=0, tiled=True)
    key_grad = lax.psum_scatter(key_terms, axes, scatter_dimension=0, tiled=True)
    return attns[0], query_grads[0], key_grad.astype(jnp.float32), value_grad.astype(jnp.float32)


def per_device(queries, grad_out, key_rows, value_rows, doc_starts):
    kv_count = key_rows.shape[1] // HEAD_DIM
    split = lax.axis_size("dp") == 2 and kv_count % 2 == 0
    body = by_head if split else by_rows
    attn, query_grad, key_grad, value_grad = body(
        queries[0], grad_out[0], key_rows, value_rows, doc_starts
    )
    return attn[None], query_grad[None], key_grad, value_grad


def solution(mesh):
    rows = P("depth", ("groups", "dp"), "heads")
    shared = P(("groups", "depth", "dp"), "heads")
    return jax.shard_map(
        per_device,
        mesh=mesh,
        in_specs=(rows, rows, shared, shared, P("groups")),
        out_specs=(rows, rows, shared, shared),
        check_vma=False,
    )
```

```python
import functools
import math

import jax
import jax.numpy as jnp
from jax import lax
from jax.experimental import pallas as pl
from jax.experimental.pallas import tpu as pltpu
from jax.sharding import PartitionSpec as P

HEAD_DIM = 128
QB = 128
GROUP = 5
GW = GROUP * HEAD_DIM
NEG_FILL = -1e30
VALUE_TILES = (4, 2, 6)
QUERY_TILES = (4, 2, 4)
SCALE = HEAD_DIM ** -0.5
SCALE2 = SCALE * math.log2(math.e)
NT = (((1,), (1,)), ((), ()))
TN = (((0,), (0,)), ((), ()))
VMEM_LIMIT = 56 * 1024 * 1024


def dot(left, right, dims=(((1,), (0,)), ((), ()))):
    return lax.dot_general(left, right, dims, preferred_element_type=jnp.float32)


def stack_heads(block):
    return jnp.concatenate([block[:, g * HEAD_DIM:(g + 1) * HEAD_DIM] for g in range(GROUP)], axis=0)


def stage_rows(step, local_steps, count, refs, stacked):
    def stage(ref):
        for part in range(count):
            stacked[part] = stack_heads(ref[part * QB:(part + 1) * QB, :])

    if len(refs) == 1:
        stage(refs[0])
    else:
        for side, ref in enumerate(refs):
            pl.when(step // local_steps == side)(functools.partial(stage, ref))


def base_block(meta, step, local_steps, count):
    part = step // local_steps
    return meta[1 + part] + (step - part * local_steps) * count


def list_units(docs, base, count, width, unit_block, unit_tile):
    def add_block(part, unit):
        tiles = (base + part + width - docs[base + part]) // width

        def add_tile(tile, unit):
            unit_block[unit] = part
            unit_tile[unit] = tile
            return unit + 1

        return lax.fori_loop(0, tiles, add_tile, unit)

    return lax.fori_loop(0, count, add_block, 0)


def each_unit(units, batch, body):
    whole = units // batch

    def many(index, carry):
        body([index * batch + k for k in range(batch)])
        return carry

    lax.fori_loop(0, whole, many, 0)
    for rest in range(1, batch):
        @pl.when(units - whole * batch == rest)
        def _():
            body([whole * batch + k for k in range(rest)])


def tile_start(block, tile, width):
    return pl.multiple_of(jnp.maximum((block + 1 - width * (tile + 1)) * QB, 0), QB)


def fill_masks(mask_ref, width):
    key_pos = lax.broadcasted_iota(jnp.int32, (width * QB, QB), 0)
    query_pos = lax.broadcasted_iota(jnp.int32, (width * QB, QB), 1)
    for upper in range(1, width + 1):
        for diagonal in range(2):
            for lower in range(width):
                allowed = (key_pos >= lower * QB) & (key_pos < upper * QB)
                if diagonal:
                    allowed &= key_pos <= query_pos + (upper - 1) * QB
                index = ((upper - 1) * 2 + diagonal) * width + lower
                mask_ref[index] = jnp.where(allowed, 0.0, NEG_FILL)


def tile_bias(docs, block, tile, start, width, mask_ref):
    start_block = jnp.maximum(block + 1 - width * (tile + 1), 0)
    upper = block - width * tile - start_block
    lower = jnp.clip(docs[block] - start_block, 0, width - 1)
    diagonal = jnp.where(tile == 0, 1, 0)
    bias = mask_ref[(upper * 2 + diagonal) * width + lower]
    return jnp.concatenate([bias] * GROUP, axis=1)


def value_kernel(local_steps, parts, count, width, batch, meta, docs, *refs):
    queries, refs = refs[:parts], refs[parts:]
    grads, refs = refs[:parts], refs[parts:]
    key_ref, total_ref, out_ref, value_sum, score_store, query, grad, best_ref, sum_ref, mask_ref = refs[:10]
    unit_block, unit_tile = refs[10:]
    step = pl.program_id(1)
    span = width * QB
    base = base_block(meta, step, local_steps, count)
    units = list_units(docs, base, count, width, unit_block, unit_tile)
    stage_rows(step, local_steps, count, queries, query)
    stage_rows(step, local_steps, count, grads, grad)
    best_ref[...] = jnp.full_like(best_ref, NEG_FILL)
    sum_ref[...] = jnp.zeros_like(sum_ref)

    @pl.when(step == 0)
    def _():
        value_sum[...] = jnp.zeros_like(value_sum)
        fill_masks(mask_ref, width)

    def score_units(which):
        scores = []
        for unit in which:
            part, tile = unit_block[unit], unit_tile[unit]
            start = tile_start(base + part, tile, width)
            bias = tile_bias(docs, base + part, tile, start, width, mask_ref)
            score = (dot(key_ref[pl.ds(start, span), :], query[part], NT) + bias) * SCALE2
            score_store[unit] = score
            scores.append(score)
        tops = [jnp.max(score, axis=0, keepdims=True) for score in scores]
        sums = [jnp.sum(jnp.exp2(score - top), axis=0, keepdims=True) for score, top in zip(scores, tops)]
        for unit, top, total in zip(which, tops, sums):
            part = unit_block[unit]
            old = best_ref[part]
            best = jnp.maximum(old, top)
            sum_ref[part] = sum_ref[part] * jnp.exp2(old - best) + total * jnp.exp2(top - best)
            best_ref[part] = best

    each_unit(units, batch, score_units)
    total_ref[0, 0] = best_ref[...] + jnp.log2(sum_ref[...])

    def value_units(which):
        terms = []
        for unit in which:
            part = unit_block[unit]
            low = jnp.exp2(score_store[unit] - total_ref[0, 0, part]).astype(jnp.bfloat16)
            terms.append(dot(low, grad[part]))
        for unit, term in zip(which, terms):
            start = tile_start(base + unit_block[unit], unit_tile[unit], width)
            value_sum[pl.ds(start, span), :] += term

    each_unit(units, batch, value_units)

    @pl.when(step == pl.num_programs(1) - 1)
    def _():
        out_ref[...] = value_sum[...].astype(out_ref.dtype)


def query_kernel(local_steps, parts, count, width, batch, meta, docs, *refs):
    queries, refs = refs[:parts], refs[parts:]
    grads, refs = refs[:parts], refs[parts:]
    key_ref, value_ref, total_ref = refs[:3]
    refs = refs[3:]
    attns, refs = refs[:parts], refs[parts:]
    query_grads, refs = refs[:parts], refs[parts:]
    key_out, key_sum, weight_store, dot_store, query, grad, attn_sum, grad_sum, dots_ref, mask_ref = refs[:10]
    unit_block, unit_tile = refs[10:]
    step = pl.program_id(1)
    span = width * QB
    base = base_block(meta, step, local_steps, count)
    units = list_units(docs, base, count, width, unit_block, unit_tile)
    stage_rows(step, local_steps, count, queries, query)
    stage_rows(step, local_steps, count, grads, grad)
    dots_ref[...] = jnp.zeros_like(dots_ref)

    @pl.when(step == 0)
    def _():
        key_sum[...] = jnp.zeros_like(key_sum)
        fill_masks(mask_ref, width)

    def attn_units(which):
        results = []
        for unit in which:
            part, tile = unit_block[unit], unit_tile[unit]
            start = tile_start(base + part, tile, width)
            bias = tile_bias(docs, base + part, tile, start, width, mask_ref)
            scores = dot(key_ref[pl.ds(start, span), :], query[part], NT) + bias
            weights = jnp.exp2(scores * SCALE2 - total_ref[0, 0, part])
            low = weights.astype(jnp.bfloat16)
            weight_store[unit] = low
            values = value_ref[pl.ds(start, span), :]
            prob_grads = dot(values, grad[part], NT)
            dot_store[unit] = prob_grads
            results.append((dot(low, values, TN), jnp.sum(weights * prob_grads, axis=0, keepdims=True)))
        for unit, (attn, dots) in zip(which, results):
            part = unit_block[unit]
            attn_sum[part] = jnp.where(unit_tile[unit] == 0, attn, attn_sum[part] + attn)
            dots_ref[part] += dots

    each_unit(units, batch, attn_units)

    def grad_units(which):
        results = []
        for unit in which:
            part = unit_block[unit]
            start = tile_start(base + part, unit_tile[unit], width)
            score_grads = weight_store[unit] * (dot_store[unit] - dots_ref[part]).astype(jnp.bfloat16)
            results.append((
                dot(score_grads, key_ref[pl.ds(start, span), :], TN),
                dot(score_grads, query[part]),
            ))
        for unit, (query_term, key_term) in zip(which, results):
            part = unit_block[unit]
            start = tile_start(base + part, unit_tile[unit], width)
            grad_sum[part] = jnp.where(unit_tile[unit] == 0, query_term, grad_sum[part] + query_term)
            key_sum[pl.ds(start, span), :] += key_term

    each_unit(units, batch, grad_units)

    def emit(attn_ref, grad_ref):
        for part in range(count):
            rows = slice(part * QB, (part + 1) * QB)
            for g in range(GROUP):
                head = slice(g * HEAD_DIM, (g + 1) * HEAD_DIM)
                stacked = slice(g * QB, (g + 1) * QB)
                attn_ref[rows, head] = attn_sum[part, stacked].astype(jnp.bfloat16)
                grad_ref[rows, head] = (grad_sum[part, stacked] * SCALE).astype(jnp.bfloat16)

    for part in range(parts):
        if parts == 1:
            emit(attns[0], query_grads[0])
        else:
            pl.when(step // local_steps == part)(functools.partial(emit, attns[part], query_grads[part]))

    @pl.when(step == pl.num_programs(1) - 1)
    def _():
        key_out[...] = (key_sum[...] * SCALE).astype(key_out.dtype)


def max_units(seq_len, count, width):
    blocks = seq_len // QB
    return sum(-(-(blocks - k) // width) for k in range(count))


def row_specs(local_steps, parts, count):
    def own(head, step, meta, docs):
        return (jnp.minimum(step, local_steps - 1), meta[0] + head)

    def received(head, step, meta, docs):
        return (jnp.maximum(step - local_steps, 0), head)

    return [pl.BlockSpec((count * QB, GW), own), pl.BlockSpec((count * QB, GW), received)][:parts]


def kv_spec(seq_len):
    return pl.BlockSpec((seq_len, HEAD_DIM), lambda head, step, meta, docs: (0, head))


def total_spec(count):
    return pl.BlockSpec((1, 1, count, 1, GW), lambda head, step, meta, docs: (head, step, 0, 0, 0))


def run_value(meta, docs, queries, grads, keys, count, width, batch):
    parts = len(queries)
    local_steps = queries[0].shape[0] // (count * QB)
    steps = local_steps * parts
    seq_len = keys.shape[0]
    heads = keys.shape[1] // HEAD_DIM
    units = max_units(seq_len, count, width)
    return pl.pallas_call(
        functools.partial(value_kernel, local_steps, parts, count, width, batch),
        grid_spec=pltpu.PrefetchScalarGridSpec(
            num_scalar_prefetch=2,
            grid=(heads, steps),
            in_specs=row_specs(local_steps, parts, count) * 2 + [kv_spec(seq_len)],
            out_specs=[total_spec(count), kv_spec(seq_len)],
            scratch_shapes=[
                pltpu.VMEM((seq_len, HEAD_DIM), jnp.float32),
                pltpu.VMEM((units, width * QB, GW), jnp.float32),
                pltpu.VMEM((count, GW, HEAD_DIM), jnp.bfloat16),
                pltpu.VMEM((count, GW, HEAD_DIM), jnp.bfloat16),
                pltpu.VMEM((count, 1, GW), jnp.float32),
                pltpu.VMEM((count, 1, GW), jnp.float32),
                pltpu.VMEM((2 * width * width, width * QB, QB), jnp.float32),
                pltpu.SMEM((units,), jnp.int32),
                pltpu.SMEM((units,), jnp.int32),
            ],
        ),
        out_shape=[
            jax.ShapeDtypeStruct((heads, steps, count, 1, GW), jnp.float32),
            jax.ShapeDtypeStruct(keys.shape, jnp.bfloat16),
        ],
        compiler_params=pltpu.CompilerParams(vmem_limit_bytes=VMEM_LIMIT),
        name="value_grad",
    )(meta, docs, *queries, *grads, keys)


def run_query(meta, docs, queries, grads, keys, values, totals, count, width, batch):
    parts = len(queries)
    local_steps = queries[0].shape[0] // (count * QB)
    steps = local_steps * parts
    seq_len = keys.shape[0]
    heads = keys.shape[1] // HEAD_DIM
    units = max_units(seq_len, count, width)
    rows = row_specs(local_steps, parts, count)
    shapes = [jax.ShapeDtypeStruct(q.shape, jnp.bfloat16) for q in queries]
    outs = pl.pallas_call(
        functools.partial(query_kernel, local_steps, parts, count, width, batch),
        grid_spec=pltpu.PrefetchScalarGridSpec(
            num_scalar_prefetch=2,
            grid=(heads, steps),
            in_specs=rows * 2 + [kv_spec(seq_len), kv_spec(seq_len), total_spec(count)],
            out_specs=rows * 2 + [kv_spec(seq_len)],
            scratch_shapes=[
                pltpu.VMEM((seq_len, HEAD_DIM), jnp.float32),
                pltpu.VMEM((units, width * QB, GW), jnp.bfloat16),
                pltpu.VMEM((units, width * QB, GW), jnp.float32),
                pltpu.VMEM((count, GW, HEAD_DIM), jnp.bfloat16),
                pltpu.VMEM((count, GW, HEAD_DIM), jnp.bfloat16),
                pltpu.VMEM((count, GW, HEAD_DIM), jnp.float32),
                pltpu.VMEM((count, GW, HEAD_DIM), jnp.float32),
                pltpu.VMEM((count, 1, GW), jnp.float32),
                pltpu.VMEM((2 * width * width, width * QB, QB), jnp.float32),
                pltpu.SMEM((units,), jnp.int32),
                pltpu.SMEM((units,), jnp.int32),
            ],
        ),
        out_shape=shapes * 2 + [jax.ShapeDtypeStruct(keys.shape, jnp.bfloat16)],
        compiler_params=pltpu.CompilerParams(vmem_limit_bytes=VMEM_LIMIT),
        name="query_grad",
    )(meta, docs, *queries, *grads, keys, values, totals)
    return outs[:parts], outs[parts:2 * parts], outs[-1]


def head_columns(rows, which, width):
    return lax.dynamic_slice(rows, (0, which * width), (rows.shape[0], width))


def swap_cores(array):
    return lax.ppermute(array, "dp", [(0, 1), (1, 0)])


def exchange(array):
    return lax.all_to_all(array, ("depth", "dp"), 0, 0, tiled=True)


def pack_heads(rows, depth_count):
    shard, width = rows.shape
    sides = jnp.transpose(rows.reshape(shard, 2, width // 2), (1, 0, 2))
    sides = jnp.broadcast_to(sides[None], (depth_count,) + sides.shape)
    return sides.reshape(2 * depth_count, shard, width // 2)


def unpack_rows(pieces):
    return pieces.reshape(pieces.shape[0] * pieces.shape[1], pieces.shape[2])


def return_terms(terms, depth_count):
    shard = terms.shape[0] // (2 * depth_count)
    return exchange(terms.reshape(2 * depth_count, shard, terms.shape[1]))


def add_terms(got):
    heads = [jnp.sum(got[side::2].astype(jnp.float32), axis=0) for side in range(2)]
    return jnp.concatenate(heads, axis=1)


def by_head(queries, grad_out, key_rows, value_rows, doc_starts):
    depth_count = lax.axis_size("depth")
    core = lax.axis_index("dp")
    local_blocks = queries.shape[0] // QB
    query_width = queries.shape[1] // 2
    heads = key_rows.shape[1] // (2 * HEAD_DIM)
    keys = unpack_rows(exchange(pack_heads(key_rows, depth_count)))
    values = unpack_rows(exchange(pack_heads(value_rows, depth_count)))
    meta = jnp.stack([core * heads, core * local_blocks, (1 - core) * local_blocks]).astype(jnp.int32)
    query_got = swap_cores(head_columns(queries, 1 - core, query_width))
    grad_got = swap_cores(head_columns(grad_out, 1 - core, query_width))
    query_parts = [queries, query_got]
    grad_parts = [grad_out, grad_got]
    totals, value_terms = run_value(meta, doc_starts, query_parts, grad_parts, keys, *VALUE_TILES)
    value_back = return_terms(value_terms, depth_count)
    attns, query_grads, key_terms = run_query(
        meta, doc_starts, query_parts, grad_parts, keys, values, totals, *QUERY_TILES
    )
    key_back = return_terms(key_terms, depth_count)
    outs = [
        lax.dynamic_update_slice(own, swap_cores(send), (0, (1 - core) * query_width))
        for own, send in (attns, query_grads)
    ]
    outs, value_grad, key_back = lax.optimization_barrier((outs, add_terms(value_back), key_back))
    return outs[0], outs[1], add_terms(key_back), value_grad


def by_rows(queries, grad_out, key_rows, value_rows, doc_starts):
    axes = ("depth", "dp")
    block = lax.axis_index("dp") * (queries.shape[0] // QB)
    keys = lax.all_gather(key_rows, axes, axis=0, tiled=True)
    values = lax.all_gather(value_rows, axes, axis=0, tiled=True)
    meta = jnp.stack([jnp.zeros_like(block), block]).astype(jnp.int32)
    totals, value_terms = run_value(meta, doc_starts, [queries], [grad_out], keys, *VALUE_TILES)
    attns, query_grads, key_terms = run_query(
        meta, doc_starts, [queries], [grad_out], keys, values, totals, *QUERY_TILES
    )
    value_grad = lax.psum_scatter(value_terms, axes, scatter_dimension=0, tiled=True)
    key_grad = lax.psum_scatter(key_terms, axes, scatter_dimension=0, tiled=True)
    return attns[0], query_grads[0], key_grad.astype(jnp.float32), value_grad.astype(jnp.float32)


def per_device(queries, grad_out, key_rows, value_rows, doc_starts):
    kv_count = key_rows.shape[1] // HEAD_DIM
    split = lax.axis_size("dp") == 2 and kv_count % 2 == 0
    body = by_head if split else by_rows
    attn, query_grad, key_grad, value_grad = body(
        queries[0], grad_out[0], key_rows, value_rows, doc_starts
    )
    return attn[None], query_grad[None], key_grad, value_grad


def solution(mesh):
    rows = P("depth", ("groups", "dp"), "heads")
    shared = P(("groups", "depth", "dp"), "heads")
    return jax.shard_map(
        per_device,
        mesh=mesh,
        in_specs=(rows, rows, shared, shared, P("groups")),
        out_specs=(rows, rows, shared, shared),
        check_vma=False,
    )
```

```python
import functools
import math

import jax
import jax.numpy as jnp
from jax import lax
from jax.experimental import pallas as pl
from jax.experimental.pallas import tpu as pltpu
from jax.sharding import PartitionSpec as P

HEAD_DIM = 128
QB = 128
GROUP = 5
GW = GROUP * HEAD_DIM
NEG_FILL = -1e30
VALUE_TILES = (4, 2, 8)
QUERY_TILES = (4, 2, 6)
SCALE = HEAD_DIM ** -0.5
SCALE2 = SCALE * math.log2(math.e)
NT = (((1,), (1,)), ((), ()))
TN = (((0,), (0,)), ((), ()))
VMEM_LIMIT = 56 * 1024 * 1024


def dot(left, right, dims=(((1,), (0,)), ((), ()))):
    return lax.dot_general(left, right, dims, preferred_element_type=jnp.float32)


def stack_heads(block):
    return jnp.concatenate([block[:, g * HEAD_DIM:(g + 1) * HEAD_DIM] for g in range(GROUP)], axis=0)


def stage_rows(step, local_steps, count, refs, stacked):
    def stage(ref):
        for part in range(count):
            stacked[part] = stack_heads(ref[part * QB:(part + 1) * QB, :])

    if len(refs) == 1:
        stage(refs[0])
    else:
        for side, ref in enumerate(refs):
            pl.when(step // local_steps == side)(functools.partial(stage, ref))


def base_block(meta, step, local_steps, count):
    part = step // local_steps
    return meta[1 + part] + (step - part * local_steps) * count


def list_units(docs, base, count, width, unit_block, unit_tile):
    def add_block(part, unit):
        tiles = (base + part + width - docs[base + part]) // width

        def add_tile(tile, unit):
            unit_block[unit] = part
            unit_tile[unit] = tile
            return unit + 1

        return lax.fori_loop(0, tiles, add_tile, unit)

    return lax.fori_loop(0, count, add_block, 0)


def each_unit(units, batch, body):
    whole = units // batch

    def many(index, carry):
        body([index * batch + k for k in range(batch)])
        return carry

    lax.fori_loop(0, whole, many, 0)
    for rest in range(1, batch):
        @pl.when(units - whole * batch == rest)
        def _():
            body([whole * batch + k for k in range(rest)])


def tile_start(block, tile, width):
    return pl.multiple_of(jnp.maximum((block + 1 - width * (tile + 1)) * QB, 0), QB)


def fill_masks(mask_ref, width):
    key_pos = lax.broadcasted_iota(jnp.int32, (width * QB, QB), 0)
    query_pos = lax.broadcasted_iota(jnp.int32, (width * QB, QB), 1)
    for upper in range(1, width + 1):
        for diagonal in range(2):
            for lower in range(width):
                allowed = (key_pos >= lower * QB) & (key_pos < upper * QB)
                if diagonal:
                    allowed &= key_pos <= query_pos + (upper - 1) * QB
                index = ((upper - 1) * 2 + diagonal) * width + lower
                mask_ref[index] = jnp.where(allowed, 0.0, NEG_FILL)


def tile_bias(docs, block, tile, start, width, mask_ref):
    start_block = jnp.maximum(block + 1 - width * (tile + 1), 0)
    upper = block - width * tile - start_block
    lower = jnp.clip(docs[block] - start_block, 0, width - 1)
    diagonal = jnp.where(tile == 0, 1, 0)
    bias = mask_ref[(upper * 2 + diagonal) * width + lower]
    return jnp.concatenate([bias] * GROUP, axis=1)


def value_kernel(local_steps, parts, count, width, batch, meta, docs, *refs):
    queries, refs = refs[:parts], refs[parts:]
    grads, refs = refs[:parts], refs[parts:]
    key_ref, total_ref, out_ref, value_sum, score_store, query, grad, best_ref, sum_ref, mask_ref = refs[:10]
    unit_block, unit_tile = refs[10:]
    step = pl.program_id(1)
    span = width * QB
    base = base_block(meta, step, local_steps, count)
    units = list_units(docs, base, count, width, unit_block, unit_tile)
    stage_rows(step, local_steps, count, queries, query)
    stage_rows(step, local_steps, count, grads, grad)
    best_ref[...] = jnp.full_like(best_ref, NEG_FILL)
    sum_ref[...] = jnp.zeros_like(sum_ref)

    @pl.when(step == 0)
    def _():
        value_sum[...] = jnp.zeros_like(value_sum)
        fill_masks(mask_ref, width)

    def score_units(which):
        scores = []
        for unit in which:
            part, tile = unit_block[unit], unit_tile[unit]
            start = tile_start(base + part, tile, width)
            bias = tile_bias(docs, base + part, tile, start, width, mask_ref)
            score = (dot(key_ref[pl.ds(start, span), :], query[part], NT) + bias) * SCALE2
            score_store[unit] = score
            scores.append(score)
        tops = [jnp.max(score, axis=0, keepdims=True) for score in scores]
        sums = [jnp.sum(jnp.exp2(score - top), axis=0, keepdims=True) for score, top in zip(scores, tops)]
        for unit, top, total in zip(which, tops, sums):
            part = unit_block[unit]
            old = best_ref[part]
            best = jnp.maximum(old, top)
            sum_ref[part] = sum_ref[part] * jnp.exp2(old - best) + total * jnp.exp2(top - best)
            best_ref[part] = best

    each_unit(units, batch, score_units)
    total_ref[0, 0] = best_ref[...] + jnp.log2(sum_ref[...])

    def value_units(which):
        terms = []
        for unit in which:
            part = unit_block[unit]
            low = jnp.exp2(score_store[unit] - total_ref[0, 0, part]).astype(jnp.bfloat16)
            terms.append(dot(low, grad[part]))
        for unit, term in zip(which, terms):
            start = tile_start(base + unit_block[unit], unit_tile[unit], width)
            value_sum[pl.ds(start, span), :] += term

    each_unit(units, batch, value_units)

    @pl.when(step == pl.num_programs(1) - 1)
    def _():
        out_ref[...] = value_sum[...].astype(out_ref.dtype)


def query_kernel(local_steps, parts, count, width, batch, meta, docs, *refs):
    queries, refs = refs[:parts], refs[parts:]
    grads, refs = refs[:parts], refs[parts:]
    key_ref, value_ref, total_ref = refs[:3]
    refs = refs[3:]
    attns, refs = refs[:parts], refs[parts:]
    query_grads, refs = refs[:parts], refs[parts:]
    key_out, key_sum, weight_store, dot_store, query, grad, attn_sum, grad_sum, dots_ref, mask_ref = refs[:10]
    unit_block, unit_tile = refs[10:]
    step = pl.program_id(1)
    span = width * QB
    base = base_block(meta, step, local_steps, count)
    units = list_units(docs, base, count, width, unit_block, unit_tile)
    stage_rows(step, local_steps, count, queries, query)
    stage_rows(step, local_steps, count, grads, grad)
    dots_ref[...] = jnp.zeros_like(dots_ref)

    @pl.when(step == 0)
    def _():
        key_sum[...] = jnp.zeros_like(key_sum)
        fill_masks(mask_ref, width)

    def attn_units(which):
        results = []
        for unit in which:
            part, tile = unit_block[unit], unit_tile[unit]
            start = tile_start(base + part, tile, width)
            bias = tile_bias(docs, base + part, tile, start, width, mask_ref)
            scores = dot(key_ref[pl.ds(start, span), :], query[part], NT) + bias
            weights = jnp.exp2(scores * SCALE2 - total_ref[0, 0, part])
            low = weights.astype(jnp.bfloat16)
            weight_store[unit] = low
            values = value_ref[pl.ds(start, span), :]
            prob_grads = dot(values, grad[part], NT)
            dot_store[unit] = prob_grads
            results.append((dot(low, values, TN), jnp.sum(weights * prob_grads, axis=0, keepdims=True)))
        for unit, (attn, dots) in zip(which, results):
            part = unit_block[unit]
            attn_sum[part] = jnp.where(unit_tile[unit] == 0, attn, attn_sum[part] + attn)
            dots_ref[part] += dots

    each_unit(units, batch, attn_units)

    def grad_units(which):
        results = []
        for unit in which:
            part = unit_block[unit]
            start = tile_start(base + part, unit_tile[unit], width)
            score_grads = weight_store[unit] * (dot_store[unit] - dots_ref[part]).astype(jnp.bfloat16)
            results.append((
                dot(score_grads, key_ref[pl.ds(start, span), :], TN),
                dot(score_grads, query[part]),
            ))
        for unit, (query_term, key_term) in zip(which, results):
            part = unit_block[unit]
            start = tile_start(base + part, unit_tile[unit], width)
            grad_sum[part] = jnp.where(unit_tile[unit] == 0, query_term, grad_sum[part] + query_term)
            key_sum[pl.ds(start, span), :] += key_term

    each_unit(units, batch, grad_units)

    def emit(attn_ref, grad_ref):
        for part in range(count):
            rows = slice(part * QB, (part + 1) * QB)
            for g in range(GROUP):
                head = slice(g * HEAD_DIM, (g + 1) * HEAD_DIM)
                stacked = slice(g * QB, (g + 1) * QB)
                attn_ref[rows, head] = attn_sum[part, stacked].astype(jnp.bfloat16)
                grad_ref[rows, head] = (grad_sum[part, stacked] * SCALE).astype(jnp.bfloat16)

    for part in range(parts):
        if parts == 1:
            emit(attns[0], query_grads[0])
        else:
            pl.when(step // local_steps == part)(functools.partial(emit, attns[part], query_grads[part]))

    @pl.when(step == pl.num_programs(1) - 1)
    def _():
        key_out[...] = (key_sum[...] * SCALE).astype(key_out.dtype)


def max_units(seq_len, count, width):
    blocks = seq_len // QB
    return sum(-(-(blocks - k) // width) for k in range(count))


def row_specs(local_steps, parts, count):
    def own(head, step, meta, docs):
        return (jnp.minimum(step, local_steps - 1), meta[0] + head)

    def received(head, step, meta, docs):
        return (jnp.maximum(step - local_steps, 0), head)

    return [pl.BlockSpec((count * QB, GW), own), pl.BlockSpec((count * QB, GW), received)][:parts]


def kv_spec(seq_len):
    return pl.BlockSpec((seq_len, HEAD_DIM), lambda head, step, meta, docs: (0, head))


def total_spec(count):
    return pl.BlockSpec((1, 1, count, 1, GW), lambda head, step, meta, docs: (head, step, 0, 0, 0))


def run_value(meta, docs, queries, grads, keys, count, width, batch):
    parts = len(queries)
    local_steps = queries[0].shape[0] // (count * QB)
    steps = local_steps * parts
    seq_len = keys.shape[0]
    heads = keys.shape[1] // HEAD_DIM
    units = max_units(seq_len, count, width)
    return pl.pallas_call(
        functools.partial(value_kernel, local_steps, parts, count, width, batch),
        grid_spec=pltpu.PrefetchScalarGridSpec(
            num_scalar_prefetch=2,
            grid=(heads, steps),
            in_specs=row_specs(local_steps, parts, count) * 2 + [kv_spec(seq_len)],
            out_specs=[total_spec(count), kv_spec(seq_len)],
            scratch_shapes=[
                pltpu.VMEM((seq_len, HEAD_DIM), jnp.float32),
                pltpu.VMEM((units, width * QB, GW), jnp.float32),
                pltpu.VMEM((count, GW, HEAD_DIM), jnp.bfloat16),
                pltpu.VMEM((count, GW, HEAD_DIM), jnp.bfloat16),
                pltpu.VMEM((count, 1, GW), jnp.float32),
                pltpu.VMEM((count, 1, GW), jnp.float32),
                pltpu.VMEM((2 * width * width, width * QB, QB), jnp.float32),
                pltpu.SMEM((units,), jnp.int32),
                pltpu.SMEM((units,), jnp.int32),
            ],
        ),
        out_shape=[
            jax.ShapeDtypeStruct((heads, steps, count, 1, GW), jnp.float32),
            jax.ShapeDtypeStruct(keys.shape, jnp.bfloat16),
        ],
        compiler_params=pltpu.CompilerParams(vmem_limit_bytes=VMEM_LIMIT),
        name="value_grad",
    )(meta, docs, *queries, *grads, keys)


def run_query(meta, docs, queries, grads, keys, values, totals, count, width, batch):
    parts = len(queries)
    local_steps = queries[0].shape[0] // (count * QB)
    steps = local_steps * parts
    seq_len = keys.shape[0]
    heads = keys.shape[1] // HEAD_DIM
    units = max_units(seq_len, count, width)
    rows = row_specs(local_steps, parts, count)
    shapes = [jax.ShapeDtypeStruct(q.shape, jnp.bfloat16) for q in queries]
    outs = pl.pallas_call(
        functools.partial(query_kernel, local_steps, parts, count, width, batch),
        grid_spec=pltpu.PrefetchScalarGridSpec(
            num_scalar_prefetch=2,
            grid=(heads, steps),
            in_specs=rows * 2 + [kv_spec(seq_len), kv_spec(seq_len), total_spec(count)],
            out_specs=rows * 2 + [kv_spec(seq_len)],
            scratch_shapes=[
                pltpu.VMEM((seq_len, HEAD_DIM), jnp.float32),
                pltpu.VMEM((units, width * QB, GW), jnp.bfloat16),
                pltpu.VMEM((units, width * QB, GW), jnp.float32),
                pltpu.VMEM((count, GW, HEAD_DIM), jnp.bfloat16),
                pltpu.VMEM((count, GW, HEAD_DIM), jnp.bfloat16),
                pltpu.VMEM((count, GW, HEAD_DIM), jnp.float32),
                pltpu.VMEM((count, GW, HEAD_DIM), jnp.float32),
                pltpu.VMEM((count, 1, GW), jnp.float32),
                pltpu.VMEM((2 * width * width, width * QB, QB), jnp.float32),
                pltpu.SMEM((units,), jnp.int32),
                pltpu.SMEM((units,), jnp.int32),
            ],
        ),
        out_shape=shapes * 2 + [jax.ShapeDtypeStruct(keys.shape, jnp.bfloat16)],
        compiler_params=pltpu.CompilerParams(vmem_limit_bytes=VMEM_LIMIT),
        name="query_grad",
    )(meta, docs, *queries, *grads, keys, values, totals)
    return outs[:parts], outs[parts:2 * parts], outs[-1]


def head_columns(rows, which, width):
    return lax.dynamic_slice(rows, (0, which * width), (rows.shape[0], width))


def swap_cores(array):
    return lax.ppermute(array, "dp", [(0, 1), (1, 0)])


def exchange(array):
    return lax.all_to_all(array, ("depth", "dp"), 0, 0, tiled=True)


def pack_heads(rows, depth_count):
    shard, width = rows.shape
    sides = jnp.transpose(rows.reshape(shard, 2, width // 2), (1, 0, 2))
    sides = jnp.broadcast_to(sides[None], (depth_count,) + sides.shape)
    return sides.reshape(2 * depth_count, shard, width // 2)


def unpack_rows(pieces):
    return pieces.reshape(pieces.shape[0] * pieces.shape[1], pieces.shape[2])


def return_terms(terms, depth_count):
    shard = terms.shape[0] // (2 * depth_count)
    return exchange(terms.reshape(2 * depth_count, shard, terms.shape[1]))


def add_terms(got):
    heads = [jnp.sum(got[side::2].astype(jnp.float32), axis=0) for side in range(2)]
    return jnp.concatenate(heads, axis=1)


def by_head(queries, grad_out, key_rows, value_rows, doc_starts):
    depth_count = lax.axis_size("depth")
    core = lax.axis_index("dp")
    local_blocks = queries.shape[0] // QB
    query_width = queries.shape[1] // 2
    heads = key_rows.shape[1] // (2 * HEAD_DIM)
    keys = unpack_rows(exchange(pack_heads(key_rows, depth_count)))
    meta = jnp.stack([core * heads, core * local_blocks, (1 - core) * local_blocks]).astype(jnp.int32)
    packed = pack_heads(value_rows, depth_count)
    query_got = swap_cores(head_columns(queries, 1 - core, query_width))
    grad_got = swap_cores(head_columns(grad_out, 1 - core, query_width))
    keys, packed, meta = lax.optimization_barrier((keys, packed, meta))
    values = unpack_rows(exchange(packed))
    query_parts = [queries, query_got]
    grad_parts = [grad_out, grad_got]
    totals, value_terms = run_value(meta, doc_starts, query_parts, grad_parts, keys, *VALUE_TILES)
    value_back = return_terms(value_terms, depth_count)
    attns, query_grads, key_terms = run_query(
        meta, doc_starts, query_parts, grad_parts, keys, values, totals, *QUERY_TILES
    )
    key_back = return_terms(key_terms, depth_count)
    outs = [
        lax.dynamic_update_slice(own, swap_cores(send), (0, (1 - core) * query_width))
        for own, send in (attns, query_grads)
    ]
    outs, value_grad, key_back = lax.optimization_barrier((outs, add_terms(value_back), key_back))
    return outs[0], outs[1], add_terms(key_back), value_grad


def by_rows(queries, grad_out, key_rows, value_rows, doc_starts):
    axes = ("depth", "dp")
    block = lax.axis_index("dp") * (queries.shape[0] // QB)
    keys = lax.all_gather(key_rows, axes, axis=0, tiled=True)
    values = lax.all_gather(value_rows, axes, axis=0, tiled=True)
    meta = jnp.stack([jnp.zeros_like(block), block]).astype(jnp.int32)
    totals, value_terms = run_value(meta, doc_starts, [queries], [grad_out], keys, *VALUE_TILES)
    attns, query_grads, key_terms = run_query(
        meta, doc_starts, [queries], [grad_out], keys, values, totals, *QUERY_TILES
    )
    value_grad = lax.psum_scatter(value_terms, axes, scatter_dimension=0, tiled=True)
    key_grad = lax.psum_scatter(key_terms, axes, scatter_dimension=0, tiled=True)
    return attns[0], query_grads[0], key_grad.astype(jnp.float32), value_grad.astype(jnp.float32)


def per_device(queries, grad_out, key_rows, value_rows, doc_starts):
    kv_count = key_rows.shape[1] // HEAD_DIM
    split = lax.axis_size("dp") == 2 and kv_count % 2 == 0
    body = by_head if split else by_rows
    attn, query_grad, key_grad, value_grad = body(
        queries[0], grad_out[0], key_rows, value_rows, doc_starts
    )
    return attn[None], query_grad[None], key_grad, value_grad


def solution(mesh):
    rows = P("depth", ("groups", "dp"), "heads")
    shared = P(("groups", "depth", "dp"), "heads")
    return jax.shard_map(
        per_device,
        mesh=mesh,
        in_specs=(rows, rows, shared, shared, P("groups")),
        out_specs=(rows, rows, shared, shared),
        check_vma=False,
    )
```

```python
import functools
import math

import jax
import jax.numpy as jnp
from jax import lax
from jax.experimental import pallas as pl
from jax.experimental.pallas import tpu as pltpu
from jax.sharding import PartitionSpec as P

HEAD_DIM = 128
QB = 128
GROUP = 5
GW = GROUP * HEAD_DIM
NEG_FILL = -1e30
VALUE_TILES = (4, 2, 8)
QUERY_TILES = (4, 2, 6)
SCALE = HEAD_DIM ** -0.5
SCALE2 = SCALE * math.log2(math.e)
NT = (((1,), (1,)), ((), ()))
TN = (((0,), (0,)), ((), ()))
VMEM_LIMIT = 56 * 1024 * 1024


def dot(left, right, dims=(((1,), (0,)), ((), ()))):
    return lax.dot_general(left, right, dims, preferred_element_type=jnp.float32)


def stack_heads(block):
    return jnp.concatenate([block[:, g * HEAD_DIM:(g + 1) * HEAD_DIM] for g in range(GROUP)], axis=0)


def stage_rows(step, local_steps, count, refs, stacked):
    def stage(ref):
        for part in range(count):
            stacked[part] = stack_heads(ref[part * QB:(part + 1) * QB, :])

    if len(refs) == 1:
        stage(refs[0])
    else:
        for side, ref in enumerate(refs):
            pl.when(step // local_steps == side)(functools.partial(stage, ref))


def base_block(meta, step, local_steps, count):
    part = step // local_steps
    return meta[1 + part] + (step - part * local_steps) * count


def list_units(docs, base, count, width, unit_block, unit_tile):
    def add_block(part, unit):
        tiles = (base + part + width - docs[base + part]) // width

        def add_tile(tile, unit):
            unit_block[unit] = part
            unit_tile[unit] = tile
            return unit + 1

        return lax.fori_loop(0, tiles, add_tile, unit)

    return lax.fori_loop(0, count, add_block, 0)


def each_unit(units, batch, body):
    whole = units // batch

    def many(index, carry):
        body([index * batch + k for k in range(batch)])
        return carry

    lax.fori_loop(0, whole, many, 0)
    for rest in range(1, batch):
        @pl.when(units - whole * batch == rest)
        def _():
            body([whole * batch + k for k in range(rest)])


def tile_start(block, tile, width):
    return pl.multiple_of(jnp.maximum((block + 1 - width * (tile + 1)) * QB, 0), QB)


def fill_masks(mask_ref, width):
    key_pos = lax.broadcasted_iota(jnp.int32, (width * QB, QB), 0)
    query_pos = lax.broadcasted_iota(jnp.int32, (width * QB, QB), 1)
    for upper in range(1, width + 1):
        for diagonal in range(2):
            for lower in range(width):
                allowed = (key_pos >= lower * QB) & (key_pos < upper * QB)
                if diagonal:
                    allowed &= key_pos <= query_pos + (upper - 1) * QB
                index = ((upper - 1) * 2 + diagonal) * width + lower
                mask_ref[index] = jnp.where(allowed, 0.0, NEG_FILL)


def tile_bias(docs, block, tile, start, width, mask_ref):
    start_block = jnp.maximum(block + 1 - width * (tile + 1), 0)
    upper = block - width * tile - start_block
    lower = jnp.clip(docs[block] - start_block, 0, width - 1)
    diagonal = jnp.where(tile == 0, 1, 0)
    bias = mask_ref[(upper * 2 + diagonal) * width + lower]
    return jnp.concatenate([bias] * GROUP, axis=1)


def value_kernel(local_steps, parts, count, width, batch, meta, docs, *refs):
    queries, refs = refs[:parts], refs[parts:]
    grads, refs = refs[:parts], refs[parts:]
    key_ref, total_ref, out_ref, value_sum, score_store, query, grad, best_ref, sum_ref, mask_ref = refs[:10]
    unit_block, unit_tile = refs[10:]
    step = pl.program_id(1)
    span = width * QB
    base = base_block(meta, step, local_steps, count)
    units = list_units(docs, base, count, width, unit_block, unit_tile)
    stage_rows(step, local_steps, count, queries, query)
    stage_rows(step, local_steps, count, grads, grad)
    best_ref[...] = jnp.full_like(best_ref, NEG_FILL)
    sum_ref[...] = jnp.zeros_like(sum_ref)

    @pl.when(step == 0)
    def _():
        value_sum[...] = jnp.zeros_like(value_sum)
        fill_masks(mask_ref, width)

    def score_units(which):
        scores = []
        for unit in which:
            part, tile = unit_block[unit], unit_tile[unit]
            start = tile_start(base + part, tile, width)
            bias = tile_bias(docs, base + part, tile, start, width, mask_ref)
            score = (dot(key_ref[pl.ds(start, span), :], query[part], NT) + bias) * SCALE2
            score_store[unit] = score
            scores.append(score)
        tops = [jnp.max(score, axis=0, keepdims=True) for score in scores]
        sums = [jnp.sum(jnp.exp2(score - top), axis=0, keepdims=True) for score, top in zip(scores, tops)]
        for unit, top, total in zip(which, tops, sums):
            part = unit_block[unit]
            old = best_ref[part]
            best = jnp.maximum(old, top)
            sum_ref[part] = sum_ref[part] * jnp.exp2(old - best) + total * jnp.exp2(top - best)
            best_ref[part] = best

    each_unit(units, batch, score_units)
    total_ref[0, 0] = best_ref[...] + jnp.log2(sum_ref[...])

    def value_units(which):
        terms = []
        for unit in which:
            part = unit_block[unit]
            low = jnp.exp2(score_store[unit] - total_ref[0, 0, part]).astype(jnp.bfloat16)
            terms.append(dot(low, grad[part]))
        for unit, term in zip(which, terms):
            start = tile_start(base + unit_block[unit], unit_tile[unit], width)
            value_sum[pl.ds(start, span), :] += term

    each_unit(units, batch, value_units)

    @pl.when(step == pl.num_programs(1) - 1)
    def _():
        out_ref[...] = value_sum[...].astype(out_ref.dtype)


def query_kernel(local_steps, parts, count, width, batch, meta, docs, *refs):
    queries, refs = refs[:parts], refs[parts:]
    grads, refs = refs[:parts], refs[parts:]
    key_ref, value_ref, total_ref = refs[:3]
    refs = refs[3:]
    attns, refs = refs[:parts], refs[parts:]
    query_grads, refs = refs[:parts], refs[parts:]
    key_out, key_sum, weight_store, dot_store, query, grad, attn_sum, grad_sum, dots_ref, mask_ref = refs[:10]
    unit_block, unit_tile = refs[10:]
    step = pl.program_id(1)
    span = width * QB
    base = base_block(meta, step, local_steps, count)
    units = list_units(docs, base, count, width, unit_block, unit_tile)
    stage_rows(step, local_steps, count, queries, query)
    stage_rows(step, local_steps, count, grads, grad)
    dots_ref[...] = jnp.zeros_like(dots_ref)

    @pl.when(step == 0)
    def _():
        key_sum[...] = jnp.zeros_like(key_sum)
        fill_masks(mask_ref, width)

    def attn_units(which):
        results = []
        for unit in which:
            part, tile = unit_block[unit], unit_tile[unit]
            start = tile_start(base + part, tile, width)
            bias = tile_bias(docs, base + part, tile, start, width, mask_ref)
            scores = dot(key_ref[pl.ds(start, span), :], query[part], NT) + bias
            weights = jnp.exp2(scores * SCALE2 - total_ref[0, 0, part])
            low = weights.astype(jnp.bfloat16)
            weight_store[unit] = low
            values = value_ref[pl.ds(start, span), :]
            prob_grads = dot(values, grad[part], NT)
            dot_store[unit] = prob_grads
            results.append((dot(low, values, TN), jnp.sum(weights * prob_grads, axis=0, keepdims=True)))
        for unit, (attn, dots) in zip(which, results):
            part = unit_block[unit]
            attn_sum[part] = jnp.where(unit_tile[unit] == 0, attn, attn_sum[part] + attn)
            dots_ref[part] += dots

    each_unit(units, batch, attn_units)

    def grad_units(which):
        results = []
        for unit in which:
            part = unit_block[unit]
            start = tile_start(base + part, unit_tile[unit], width)
            score_grads = weight_store[unit] * (dot_store[unit] - dots_ref[part]).astype(jnp.bfloat16)
            results.append((
                dot(score_grads, key_ref[pl.ds(start, span), :], TN),
                dot(score_grads, query[part]),
            ))
        for unit, (query_term, key_term) in zip(which, results):
            part = unit_block[unit]
            start = tile_start(base + part, unit_tile[unit], width)
            grad_sum[part] = jnp.where(unit_tile[unit] == 0, query_term, grad_sum[part] + query_term)
            key_sum[pl.ds(start, span), :] += key_term

    each_unit(units, batch, grad_units)

    def emit(attn_ref, grad_ref):
        for part in range(count):
            rows = slice(part * QB, (part + 1) * QB)
            for g in range(GROUP):
                head = slice(g * HEAD_DIM, (g + 1) * HEAD_DIM)
                stacked = slice(g * QB, (g + 1) * QB)
                attn_ref[rows, head] = attn_sum[part, stacked].astype(jnp.bfloat16)
                grad_ref[rows, head] = (grad_sum[part, stacked] * SCALE).astype(jnp.bfloat16)

    for part in range(parts):
        if parts == 1:
            emit(attns[0], query_grads[0])
        else:
            pl.when(step // local_steps == part)(functools.partial(emit, attns[part], query_grads[part]))

    @pl.when(step == pl.num_programs(1) - 1)
    def _():
        key_out[...] = (key_sum[...] * SCALE).astype(key_out.dtype)


def max_units(seq_len, count, width):
    blocks = seq_len // QB
    return sum(-(-(blocks - k) // width) for k in range(count))


def row_specs(local_steps, parts, count):
    def own(head, step, meta, docs):
        return (jnp.minimum(step, local_steps - 1), meta[0] + head)

    def received(head, step, meta, docs):
        return (jnp.maximum(step - local_steps, 0), head)

    return [pl.BlockSpec((count * QB, GW), own), pl.BlockSpec((count * QB, GW), received)][:parts]


def kv_spec(seq_len):
    return pl.BlockSpec((seq_len, HEAD_DIM), lambda head, step, meta, docs: (0, head))


def total_spec(count):
    return pl.BlockSpec((1, 1, count, 1, GW), lambda head, step, meta, docs: (head, step, 0, 0, 0))


def run_value(meta, docs, queries, grads, keys, count, width, batch):
    parts = len(queries)
    local_steps = queries[0].shape[0] // (count * QB)
    steps = local_steps * parts
    seq_len = keys.shape[0]
    heads = keys.shape[1] // HEAD_DIM
    units = max_units(seq_len, count, width)
    return pl.pallas_call(
        functools.partial(value_kernel, local_steps, parts, count, width, batch),
        grid_spec=pltpu.PrefetchScalarGridSpec(
            num_scalar_prefetch=2,
            grid=(heads, steps),
            in_specs=row_specs(local_steps, parts, count) * 2 + [kv_spec(seq_len)],
            out_specs=[total_spec(count), kv_spec(seq_len)],
            scratch_shapes=[
                pltpu.VMEM((seq_len, HEAD_DIM), jnp.float32),
                pltpu.VMEM((units, width * QB, GW), jnp.float32),
                pltpu.VMEM((count, GW, HEAD_DIM), jnp.bfloat16),
                pltpu.VMEM((count, GW, HEAD_DIM), jnp.bfloat16),
                pltpu.VMEM((count, 1, GW), jnp.float32),
                pltpu.VMEM((count, 1, GW), jnp.float32),
                pltpu.VMEM((2 * width * width, width * QB, QB), jnp.float32),
                pltpu.SMEM((units,), jnp.int32),
                pltpu.SMEM((units,), jnp.int32),
            ],
        ),
        out_shape=[
            jax.ShapeDtypeStruct((heads, steps, count, 1, GW), jnp.float32),
            jax.ShapeDtypeStruct(keys.shape, jnp.bfloat16),
        ],
        compiler_params=pltpu.CompilerParams(vmem_limit_bytes=VMEM_LIMIT),
        name="value_grad",
    )(meta, docs, *queries, *grads, keys)


def run_query(meta, docs, queries, grads, keys, values, totals, count, width, batch):
    parts = len(queries)
    local_steps = queries[0].shape[0] // (count * QB)
    steps = local_steps * parts
    seq_len = keys.shape[0]
    heads = keys.shape[1] // HEAD_DIM
    units = max_units(seq_len, count, width)
    rows = row_specs(local_steps, parts, count)
    shapes = [jax.ShapeDtypeStruct(q.shape, jnp.bfloat16) for q in queries]
    outs = pl.pallas_call(
        functools.partial(query_kernel, local_steps, parts, count, width, batch),
        grid_spec=pltpu.PrefetchScalarGridSpec(
            num_scalar_prefetch=2,
            grid=(heads, steps),
            in_specs=rows * 2 + [kv_spec(seq_len), kv_spec(seq_len), total_spec(count)],
            out_specs=rows * 2 + [kv_spec(seq_len)],
            scratch_shapes=[
                pltpu.VMEM((seq_len, HEAD_DIM), jnp.float32),
                pltpu.VMEM((units, width * QB, GW), jnp.bfloat16),
                pltpu.VMEM((units, width * QB, GW), jnp.float32),
                pltpu.VMEM((count, GW, HEAD_DIM), jnp.bfloat16),
                pltpu.VMEM((count, GW, HEAD_DIM), jnp.bfloat16),
                pltpu.VMEM((count, GW, HEAD_DIM), jnp.float32),
                pltpu.VMEM((count, GW, HEAD_DIM), jnp.float32),
                pltpu.VMEM((count, 1, GW), jnp.float32),
                pltpu.VMEM((2 * width * width, width * QB, QB), jnp.float32),
                pltpu.SMEM((units,), jnp.int32),
                pltpu.SMEM((units,), jnp.int32),
            ],
        ),
        out_shape=shapes * 2 + [jax.ShapeDtypeStruct(keys.shape, jnp.bfloat16)],
        compiler_params=pltpu.CompilerParams(vmem_limit_bytes=VMEM_LIMIT),
        name="query_grad",
    )(meta, docs, *queries, *grads, keys, values, totals)
    return outs[:parts], outs[parts:2 * parts], outs[-1]


def head_columns(rows, which, width):
    return lax.dynamic_slice(rows, (0, which * width), (rows.shape[0], width))


def swap_cores(array):
    return lax.ppermute(array, "dp", [(0, 1), (1, 0)])


def exchange(array):
    return lax.all_to_all(array, ("depth", "dp"), 0, 0, tiled=True)


def pack_kernel(rows_ref, out_ref):
    width = rows_ref.shape[1] // 2
    for target in range(out_ref.shape[0]):
        side = target % 2
        out_ref[target] = rows_ref[:, side * width:(side + 1) * width]


def pack_heads(rows, depth_count):
    shard, width = rows.shape
    return pl.pallas_call(
        pack_kernel,
        out_shape=jax.ShapeDtypeStruct((2 * depth_count, shard, width // 2), rows.dtype),
        name="pack_heads",
    )(rows)


def unpack_rows(pieces):
    return pieces.reshape(pieces.shape[0] * pieces.shape[1], pieces.shape[2])


def return_terms(terms, depth_count):
    shard = terms.shape[0] // (2 * depth_count)
    return exchange(terms.reshape(2 * depth_count, shard, terms.shape[1]))


def add_terms(got):
    heads = [jnp.sum(got[side::2].astype(jnp.float32), axis=0) for side in range(2)]
    return jnp.concatenate(heads, axis=1)


def by_head(queries, grad_out, key_rows, value_rows, doc_starts):
    depth_count = lax.axis_size("depth")
    core = lax.axis_index("dp")
    local_blocks = queries.shape[0] // QB
    query_width = queries.shape[1] // 2
    heads = key_rows.shape[1] // (2 * HEAD_DIM)
    keys = unpack_rows(exchange(pack_heads(key_rows, depth_count)))
    packed_values = pack_heads(value_rows, depth_count)
    meta = jnp.stack([core * heads, core * local_blocks, (1 - core) * local_blocks]).astype(jnp.int32)
    query_got = swap_cores(head_columns(queries, 1 - core, query_width))
    grad_got = swap_cores(head_columns(grad_out, 1 - core, query_width))
    keys, packed_values, meta = lax.optimization_barrier((keys, packed_values, meta))
    values = unpack_rows(exchange(packed_values))
    query_got, grad_got = [
        pltpu.with_memory_space_constraint(rows, pltpu.HBM) for rows in (query_got, grad_got)
    ]
    query_parts = [queries, query_got]
    grad_parts = [grad_out, grad_got]
    totals, value_terms = run_value(meta, doc_starts, query_parts, grad_parts, keys, *VALUE_TILES)
    value_back = return_terms(value_terms, depth_count)
    attns, query_grads, key_terms = run_query(
        meta, doc_starts, query_parts, grad_parts, keys, values, totals, *QUERY_TILES
    )
    key_back = return_terms(key_terms, depth_count)
    outs = [
        lax.dynamic_update_slice(own, swap_cores(send), (0, (1 - core) * query_width))
        for own, send in (attns, query_grads)
    ]
    outs, value_grad, key_back = lax.optimization_barrier((outs, add_terms(value_back), key_back))
    return outs[0], outs[1], add_terms(key_back), value_grad


def by_rows(queries, grad_out, key_rows, value_rows, doc_starts):
    axes = ("depth", "dp")
    block = lax.axis_index("dp") * (queries.shape[0] // QB)
    keys = lax.all_gather(key_rows, axes, axis=0, tiled=True)
    values = lax.all_gather(value_rows, axes, axis=0, tiled=True)
    meta = jnp.stack([jnp.zeros_like(block), block]).astype(jnp.int32)
    totals, value_terms = run_value(meta, doc_starts, [queries], [grad_out], keys, *VALUE_TILES)
    attns, query_grads, key_terms = run_query(
        meta, doc_starts, [queries], [grad_out], keys, values, totals, *QUERY_TILES
    )
    value_grad = lax.psum_scatter(value_terms, axes, scatter_dimension=0, tiled=True)
    key_grad = lax.psum_scatter(key_terms, axes, scatter_dimension=0, tiled=True)
    return attns[0], query_grads[0], key_grad.astype(jnp.float32), value_grad.astype(jnp.float32)


def per_device(queries, grad_out, key_rows, value_rows, doc_starts):
    kv_count = key_rows.shape[1] // HEAD_DIM
    split = lax.axis_size("dp") == 2 and kv_count % 2 == 0
    body = by_head if split else by_rows
    attn, query_grad, key_grad, value_grad = body(
        queries[0], grad_out[0], key_rows, value_rows, doc_starts
    )
    return attn[None], query_grad[None], key_grad, value_grad


def solution(mesh):
    rows = P("depth", ("groups", "dp"), "heads")
    shared = P(("groups", "depth", "dp"), "heads")
    return jax.shard_map(
        per_device,
        mesh=mesh,
        in_specs=(rows, rows, shared, shared, P("groups")),
        out_specs=(rows, rows, shared, shared),
        check_vma=False,
    )
```
